256 devices in a mesh: depth: 4 (over x), tile: 64 (over y, z, core).
Axes of the slice: x: 4, y: 4, z: 8, core: 2. Of those that a mesh axis runs over, the one named last changes fastest.
Arguments:
- source: bfloat16 [128, 2, 128, 256], P('tile'), may hold values from -6 to 6
- anchors: int32 [128], P('tile'), may hold values from -256 to 16128, as said below
- counts: int32 [4], P('depth'), may hold values from 1 to 3, 8 in all
- reflect: bfloat16 [4, 3, 128, 16384], P('depth', None, None, 'tile'), may hold values from -0.3984375 to 0.3984375
- lateral_x: bfloat16 [4, 3, 2, 128, 128], P('depth'), may hold values from -0.375 to 0.375
- lateral_y: bfloat16 [4, 3, 2, 256, 256], P('depth'), may hold values from -0.25 to 0.25
Outputs:
- image: float32 [4, 3, 128, 16384], P('depth', None, None, 'tile')
The draws below stay inside these ranges and needn't reach their ends.
Inputs may be any that keep to these rules, and one draw needn't show every extreme that they name: `anchors`: the shots held by tile index t start their aperture between (t - 1) * 256 and t * 256. The counts sum to 8; slots at or past a section's count are unused.
All inputs are finite; a program needn't handle non-finite values. No bound on the sum of `counts` on one device may be relied on, other than what follows from the above.
Results may differ from the reference program's by a relative error of at most 0.023.
Values may be sent and summed in bfloat16 or wider, within the bound.
A program may use at most 64 MiB of HBM per device.

```python
import math
import jax
import jax.numpy as jnp
import numpy as np
from jax import lax

AX = 128
AY = 256
TY = 256
LVL_MAX = 3
LEVELS = 8
SHOT_DEV = 2
SECTIONS = 4
SHOTS = 128
GY = 16384


def draw_anchors(key, part):
    owner = jnp.arange(SHOTS, dtype=jnp.int32) // SHOT_DEV
    jitter = jax.random.randint(key, (SHOTS,), 0, TY + 1, dtype=jnp.int32)
    jitter = jitter.at[0].set(0).at[SHOTS - 1].set(TY)
    return ((owner - 1) * TY + jitter).astype(jnp.int32)


def shard_levels(key, extent, split, smallest, high):
    def one(position, parts):
        draws = jax.random.uniform(jax.random.fold_in(jax.random.fold_in(key, 6), position), (parts,), jnp.float32, smallest / len(split), high / len(split))
        return jnp.repeat(jnp.exp(draws), extent[position] // parts).reshape((-1,) + (1,) * (len(extent) - position - 1))

    loudness = one(*split[0])
    for cut in split[1:]:
        loudness = loudness * one(*cut)
    return loudness


def profile(number_of, total, reach, lean):
    weights = [(1 << 20) // math.isqrt(standing ** lean) + 1 for standing in range(2, number_of + 1)]
    rest, holding = total - reach - (number_of - 1), [1] * (number_of - 1)
    while rest > 0:
        candidates = [i for i in range(number_of - 1) if holding[i] < reach]
        mass, remaining = sum([weights[i] for i in candidates]), rest
        for i in candidates:
            addition = min(reach - holding[i], max(1, remaining * weights[i] // mass), rest)
            holding[i] = holding[i] + addition
            rest = rest - addition
    return np.array([reach] + holding)


def ragged_sizes(stream_key, count, total, reach, slope):
    if count == 2:
        one = jax.random.randint(stream_key, (), max(1, total - reach), min(reach, total - 1) + 1)
        return jnp.stack([one, total - one])
    sizes = jnp.asarray(profile(count, total, reach, slope), jnp.int32)
    twos = (count - 1) // 2
    source_of, receiver = sizes[1:1 + 2 * twos:2], sizes[2:2 + 2 * twos:2]
    room = jnp.minimum(source_of - 1, reach - receiver)
    moved = jax.random.randint(jax.random.fold_in(stream_key, 1), (twos,), 0, 1 << 20) % (room + 1)
    sizes = sizes.at[1:1 + 2 * twos:2].set(source_of - moved).at[2:2 + 2 * twos:2].set(receiver + moved)
    return sizes[jax.random.permutation(jax.random.fold_in(stream_key, 2), count)]


def gaussian(own_key, extent, scale, bound, split=(), kind=jnp.bfloat16):
    factor_of = shard_levels(own_key, extent, split, -0.22, 0.18) if split else 1.0
    values = jax.random.normal(own_key, extent, jnp.float32) * scale * factor_of
    return jnp.minimum(jnp.maximum(values, -bound), bound).astype(kind)


def setup_inputs(seed: int = 0) -> dict:
    keys = jax.random.split(jax.random.key(seed), 7)
    return {
        "source": gaussian(keys[0], (SHOTS, 2, AX, AY), 1.0, 6.0, ((0, 64),)),
        "anchors": draw_anchors(jax.random.fold_in(keys[6], 71), 0),
        "counts": ragged_sizes(keys[2], SECTIONS, LEVELS, LVL_MAX, 0).astype(jnp.int32),
        "reflect": jnp.clip(jax.random.uniform(keys[3], (SECTIONS, LVL_MAX, AX, GY), jnp.float32, -0.3984375, 0.3984375) * shard_levels(keys[3], (SECTIONS, LVL_MAX, AX, GY), ((0, 4), (3, 64)), -0.4, 0.0), -0.3984375, 0.3984375).astype(jnp.bfloat16),
        "lateral_x": gaussian(keys[4], (SECTIONS, LVL_MAX, 2, AX, AX), (2 * AX) ** -0.5, 0.375, ((0, 4),)),
        "lateral_y": gaussian(keys[5], (SECTIONS, LVL_MAX, 2, AY, AY), (2 * AY) ** -0.5, 0.25, ((0, 4),)),
    }


def pair_product(einsum_form, first_pair, second_pair):
    real_part = jnp.einsum(einsum_form, first_pair[0], second_pair[0]) - jnp.einsum(einsum_form, first_pair[1], second_pair[1])
    imag_part = jnp.einsum(einsum_form, first_pair[0], second_pair[1]) + jnp.einsum(einsum_form, first_pair[1], second_pair[0])
    return jnp.stack([real_part, imag_part])


def settle(values):
    return lax.optimization_barrier(values.astype(jnp.bfloat16)).astype(jnp.float32)


def one_shot(source_shot, anchor, padded, lateral_x, lateral_y, counts):
    windows = lax.dynamic_slice_in_dim(padded, (anchor + TY).astype(jnp.int32), AY, 3).astype(jnp.float32)
    op_first = lateral_x.astype(jnp.float32)
    op_second = lateral_y.astype(jnp.float32)
    wavefield = source_shot
    stored = []
    for section in range(SECTIONS):
        for level_slot in range(LVL_MAX):
            stored.append(wavefield)
            current = wavefield.astype(jnp.float32)
            scaled = settle((1.0 + windows[section, level_slot]) * current)
            middle = settle(pair_product("ab,by->ay", op_first[section, level_slot], scaled))
            moved = pair_product("xb,ab->xa", middle, op_second[section, level_slot]).astype(jnp.bfloat16)
            wavefield = jnp.where(level_slot < counts[section], moved, wavefield)
    upgoing = jnp.zeros((2, AX, AY), jnp.bfloat16)
    per_level = [None] * (SECTIONS * LVL_MAX)
    for section in reversed(range(SECTIONS)):
        for level_slot in reversed(range(LVL_MAX)):
            flat_index = section * LVL_MAX + level_slot
            downgoing = stored[flat_index].astype(jnp.float32)
            back_wave = settle(pair_product("ba,by->ay", op_first[section, level_slot], upgoing.astype(jnp.float32)))
            spread = pair_product("xb,ba->xa", back_wave, op_second[section, level_slot])
            fresh = (windows[section, level_slot] * downgoing + spread).astype(jnp.bfloat16)
            is_live = level_slot < counts[section]
            upgoing = jnp.where(is_live, fresh, upgoing)
            product_pair = downgoing * upgoing.astype(jnp.float32)
            per_level[flat_index] = jnp.where(is_live, product_pair[0] + product_pair[1], jnp.float32(0.0))
    return jnp.stack(per_level).reshape(SECTIONS, LVL_MAX, AX, AY)


def reference(source, anchors, counts, reflect, lateral_x, lateral_y):
    padded = jnp.pad(reflect, ((0, 0), (0, 0), (0, 0), (TY, TY)))

    def absorb(canvas, inputs):
        source_shot, anchor = inputs
        contribution = one_shot(source_shot, anchor, padded, lateral_x, lateral_y, counts)
        offset = (anchor + TY).astype(jnp.int32)
        placed = lax.dynamic_slice_in_dim(canvas, offset, AY, 3) + contribution
        return lax.dynamic_update_slice_in_dim(canvas, placed, offset, 3), None

    canvas = jnp.zeros((SECTIONS, LVL_MAX, AX, GY + 2 * TY), jnp.float32)
    canvas, unused = lax.scan(absorb, canvas, (source, anchors))
    return canvas[:, :, :, TY:TY + GY]
```

```python
import functools

import jax
import jax.numpy as jnp
from jax import lax
from jax.experimental import pallas as pl
from jax.experimental.pallas import tpu as pltpu
from jax.sharding import PartitionSpec as P

MESH = pl.DeviceIdType.MESH
F32 = jnp.float32
BF16 = jnp.bfloat16


def dot_nn(a, b):
    return lax.dot_general(a, b, (((1,), (0,)), ((), ())), preferred_element_type=F32)


def dot_nt(a, b):
    return lax.dot_general(a, b, (((1,), (1,)), ((), ())), preferred_element_type=F32)


def kernel(
    nx, nt,
    source, anchors, counts, reflect, lx, ly, out,
    refl_own, refl_left, lxv, yv, xb, xbt, sel_own, sel_left, win,
    down_in, down_out, up_in, up_out, stored, corr, img_out, img_in,
    local_sem, refl_send, refl_recv, down_send, down_recv, up_send, up_recv, img_send, img_recv,
):
    slots, rows, width = refl_own.shape
    shots = down_in.shape[0]
    x = lax.axis_index("depth")
    t = lax.axis_index("tile")

    def remote(src, dst, send, recv, target):
        return pltpu.make_async_remote_copy(
            src_ref=src, dst_ref=dst, send_sem=send, recv_sem=recv,
            device_id=target, device_id_type=MESH,
        )

    to_below = (jnp.minimum(x + 1, nx - 1), t)
    to_above = (jnp.maximum(x - 1, 0), t)
    to_right = (x, jnp.minimum(t + 1, nt - 1))
    to_left = (x, jnp.maximum(t - 1, 0))

    copies = [
        pltpu.make_async_copy(lx.at[0], lxv, local_sem.at[0]),
        pltpu.make_async_copy(reflect.at[0], refl_own, local_sem.at[1]),
        pltpu.make_async_copy(ly.at[0], yv, local_sem.at[2]),
    ]
    for copy in copies:
        copy.start()

    barrier = pltpu.get_barrier_semaphore()
    neighbours = (
        (lax.rem(x + 1, nx), t), (lax.rem(x + nx - 1, nx), t),
        (x, lax.rem(t + 1, nt)), (x, lax.rem(t + nt - 1, nt)),
    )
    for neighbour in neighbours:
        pl.semaphore_signal(barrier, inc=1, device_id=neighbour, device_id_type=MESH)

    refl_copies = [
        remote(reflect.at[0, l], refl_left.at[l], refl_send.at[l], refl_recv.at[l], to_right)
        for l in range(slots)
    ]
    down_copies = [
        remote(down_out.at[k], down_in.at[k], down_send.at[k], down_recv.at[k], to_below)
        for k in range(shots)
    ]
    up_copies = [
        remote(up_out.at[k], up_in.at[k], up_send.at[k], up_recv.at[k], to_above)
        for k in range(shots)
    ]
    img_copies = [
        remote(img_out.at[l], img_in.at[l], img_send.at[l], img_recv.at[l], to_left)
        for l in range(slots)
    ]
    source_copies = [
        pltpu.make_async_copy(source.at[k], down_in.at[k], local_sem.at[3 + k])
        for k in range(shots)
    ]

    @pl.when(x == 0)
    def _():
        for copy in source_copies:
            copy.start()

    pl.semaphore_wait(barrier, 4)

    @pl.when(t < nt - 1)
    def _():
        for copy in refl_copies:
            copy.start()

    level_count = counts[0]
    i_r = lax.broadcasted_iota(jnp.int32, (rows, rows), 0)
    i_c = lax.broadcasted_iota(jnp.int32, (rows, rows), 1)
    eye_x = (i_r == i_c).astype(F32)
    j_r = lax.broadcasted_iota(jnp.int32, (width, width), 0)
    j_c = lax.broadcasted_iota(jnp.int32, (width, width), 1)
    live = [(level_count > l).astype(F32) for l in range(slots)]
    copies[0].wait()
    for l in range(slots):
        x_re = lxv[l, 0].astype(F32)
        x_im = lxv[l, 1].astype(F32)
        if l > 0:
            x_re = x_re * live[l] + eye_x * (1.0 - live[l])
            x_im = x_im * live[l]
        xb[l, :rows, :rows] = x_re.astype(BF16)
        xb[l, :rows, rows:] = (-x_im).astype(BF16)
        xb[l, rows:, :rows] = x_im.astype(BF16)
        xb[l, rows:, rows:] = x_re.astype(BF16)
        x_ret = x_re.T
        x_imt = x_im.T
        xbt[l, :rows, :rows] = x_ret.astype(BF16)
        xbt[l, :rows, rows:] = (-x_imt).astype(BF16)
        xbt[l, rows:, :rows] = x_imt.astype(BF16)
        xbt[l, rows:, rows:] = x_ret.astype(BF16)
    copies[2].wait()
    eye_y = (j_r == j_c).astype(F32)
    for l in range(1, slots):
        yv[l, 0] = (yv[l, 0].astype(F32) * live[l] + eye_y * (1.0 - live[l])).astype(BF16)
        yv[l, 1] = (yv[l, 1].astype(F32) * live[l]).astype(BF16)

    for k in range(shots):
        offset = anchors[k] - (t - 1) * width
        sel_left[:, k * width : (k + 1) * width] = (j_r - j_c == offset).astype(BF16)
        sel_own[:, k * width : (k + 1) * width] = (j_r - j_c == offset - width).astype(BF16)
    copies[1].wait()
    for l in range(slots):
        win[l] = dot_nn(refl_own[l], sel_own[...]) * live[l]

    @pl.when(t == 0)
    def _():
        refl_left[...] = jnp.zeros_like(refl_left)

    for l in range(slots):
        @pl.when(t > 0)
        def _(l=l):
            refl_copies[l].wait_recv()
        win[l] += dot_nn(refl_left[l], sel_left[...]) * live[l]

    def window(k, l):
        return win[l, :, k * width : (k + 1) * width]

    def descend(k):
        @pl.when(x == 0)
        def _():
            source_copies[k].wait()

        @pl.when(x > 0)
        def _():
            down_copies[k].wait_recv()

        for l in range(slots):
            gain = 1.0 + window(k, l)
            entering = down_in.at[k] if l == 0 else stored.at[k, l - 1]
            scaled = jnp.concatenate(
                [
                    (gain * entering[:rows].astype(F32)).astype(BF16),
                    (gain * entering[rows:].astype(F32)).astype(BF16),
                ],
                axis=0,
            )
            middle = dot_nn(xb[l], scaled).astype(BF16)
            by_re = dot_nt(middle, yv[l, 0])
            by_im = dot_nt(middle, yv[l, 1])
            leaving = stored.at[k, l] if l < slots - 1 else down_out.at[k]
            leaving[:rows] = (by_re[:rows] - by_im[rows:]).astype(BF16)
            leaving[rows:] = (by_im[:rows] + by_re[rows:]).astype(BF16)

        @pl.when(x < nx - 1)
        def _():
            down_copies[k].start()

    def ascend(k, last):
        if last:
            up_in[k] = jnp.zeros_like(up_in[k])
        else:
            up_copies[k].wait_recv()
        upgoing = up_in[k]
        for l in reversed(range(slots)):
            back = dot_nn(xbt[l], upgoing).astype(BF16)
            by_re = dot_nn(back, yv[l, 0])
            by_im = dot_nn(back, yv[l, 1])
            downward = down_in.at[k] if l == 0 else stored.at[k, l - 1]
            gain = window(k, l)
            d_re = downward[:rows].astype(F32)
            d_im = downward[rows:].astype(F32)
            u_re = (gain * d_re + (by_re[:rows] - by_im[rows:])).astype(BF16)
            u_im = (gain * d_im + (by_im[:rows] + by_re[rows:])).astype(BF16)
            if l > 0:
                upgoing = jnp.concatenate([u_re, u_im], axis=0)
            else:
                up_out[k, :rows] = u_re
                up_out[k, rows:] = u_im
            product = (d_re * u_re.astype(F32) + d_im * u_im.astype(F32)) * live[l]
            corr[l, :, k * width : (k + 1) * width] = product.astype(BF16)

        @pl.when(x > 0)
        def _():
            up_copies[k].start()

    @pl.when(x < nx - 1)
    def _():
        for k in range(shots):
            descend(k)
        for k in range(shots):
            ascend(k, False)

    @pl.when(x == nx - 1)
    def _():
        for k in range(shots):
            descend(k)
            ascend(k, True)

    for l in reversed(range(slots)):
        img_out[l] = dot_nt(corr[l], sel_left[...]).astype(BF16)

        @pl.when(t > 0)
        def _(l=l):
            img_copies[l].start()

    for l in reversed(range(slots)):
        out[0, l] = dot_nt(corr[l], sel_own[...])

    @pl.when(t < nt - 1)
    def _():
        for l in reversed(range(slots)):
            img_copies[l].wait_recv()
            out[0, l] += img_in[l].astype(F32)

    @pl.when(t < nt - 1)
    def _():
        for copy in refl_copies:
            copy.wait_send()

    @pl.when(x < nx - 1)
    def _():
        for copy in down_copies:
            copy.wait_send()

    @pl.when(x > 0)
    def _():
        for copy in up_copies:
            copy.wait_send()

    @pl.when(t > 0)
    def _():
        for copy in img_copies:
            copy.wait_send()


def solution(mesh):
    nx, nt = mesh.shape["depth"], mesh.shape["tile"]

    def on_device(source, anchors, counts, reflect, lateral_x, lateral_y):
        shots, _, rows, width = source.shape
        slots = reflect.shape[1]
        any_spec = pl.BlockSpec(memory_space=pl.ANY)
        smem = pl.BlockSpec(memory_space=pltpu.SMEM)
        wave = (shots, 2 * rows, width)
        dma = pltpu.SemaphoreType.DMA
        return pl.pallas_call(
            functools.partial(kernel, nx, nt),
            out_shape=jax.ShapeDtypeStruct((1, slots, rows, width), F32),
            in_specs=[any_spec, smem, smem, any_spec, any_spec, any_spec],
            out_specs=pl.BlockSpec(memory_space=pltpu.VMEM),
            scratch_shapes=[
                pltpu.VMEM((slots, rows, width), BF16),
                pltpu.VMEM((slots, rows, width), BF16),
                pltpu.VMEM((slots, 2, rows, rows), BF16),
                pltpu.VMEM((slots, 2, width, width), BF16),
                pltpu.VMEM((slots, 2 * rows, 2 * rows), BF16),
                pltpu.VMEM((slots, 2 * rows, 2 * rows), BF16),
                pltpu.VMEM((width, shots * width), BF16),
                pltpu.VMEM((width, shots * width), BF16),
                pltpu.VMEM((slots, rows, shots * width), F32),
                pltpu.VMEM(wave, BF16),
                pltpu.VMEM(wave, BF16),
                pltpu.VMEM(wave, BF16),
                pltpu.VMEM(wave, BF16),
                pltpu.VMEM((shots, slots - 1, 2 * rows, width), BF16),
                pltpu.VMEM((slots, rows, shots * width), BF16),
                pltpu.VMEM((slots, rows, width), BF16),
                pltpu.VMEM((slots, rows, width), BF16),
                dma((3 + shots,)),
                dma((slots,)), dma((slots,)),
                dma((shots,)), dma((shots,)),
                dma((shots,)), dma((shots,)),
                dma((slots,)), dma((slots,)),
            ],
            compiler_params=pltpu.CompilerParams(collective_id=0, has_side_effects=True),
        )(source.reshape(wave), anchors, counts, reflect, lateral_x, lateral_y)

    return jax.shard_map(
        on_device,
        mesh=mesh,
        in_specs=(
            P("tile", None, None, None),
            P("tile"),
            P("depth"),
            P("depth", None, None, "tile"),
            P("depth", None, None, None, None),
            P("depth", None, None, None, None),
        ),
        out_specs=P("depth", None, None, "tile"),
        check_vma=False,
    )
```

```python
import functools

import jax
import jax.numpy as jnp
from jax import lax
from jax.experimental import pallas as pl
from jax.experimental.pallas import tpu as pltpu
from jax.sharding import PartitionSpec as P

MESH = pl.DeviceIdType.MESH
F32 = jnp.float32
BF16 = jnp.bfloat16


def dot_nn(a, b):
    return lax.dot_general(a, b, (((1,), (0,)), ((), ())), preferred_element_type=F32)


def dot_nt(a, b):
    return lax.dot_general(a, b, (((1,), (1,)), ((), ())), preferred_element_type=F32)


def complex_dot(a_re, a_im, b_re, b_im):
    re = dot_nn(a_re, b_re) - dot_nn(a_im, b_im)
    im = dot_nn(a_re, b_im) + dot_nn(a_im, b_re)
    return re.astype(BF16), im.astype(BF16)


def kernel(
    nt,
    source, anchors_hbm, counts_hbm, reflect, lx, ly, out,
    anchors, counts, refl_own, refl_left, lxv, yv, xb, xbt, sel_own, sel_left, win,
    waves, late, early, early_out, own_x, own_y, comp_x, comp_y, comp_out_x, comp_out_y,
    corr, img_out, img_in,
    local_sem, refl_send, refl_recv, down_send, down_recv, late_send, late_recv,
    early_send, early_recv, comp_send, comp_recv, img_send, img_recv,
):
    slots, rows, width = refl_own.shape
    shots = waves.shape[0]
    x = lax.axis_index("depth")
    t = lax.axis_index("tile")

    def remote(src, dst, send, recv, target):
        return pltpu.make_async_remote_copy(
            src_ref=src, dst_ref=dst, send_sem=send, recv_sem=recv,
            device_id=target, device_id_type=MESH,
        )

    copies = [
        pltpu.make_async_copy(lx.at[0], lxv, local_sem.at[0]),
        pltpu.make_async_copy(reflect.at[0], refl_own, local_sem.at[1]),
        pltpu.make_async_copy(ly.at[0], yv, local_sem.at[2]),
        pltpu.make_async_copy(anchors_hbm, anchors, local_sem.at[3]),
        pltpu.make_async_copy(counts_hbm, counts, local_sem.at[4]),
    ]
    for copy in copies:
        copy.start()

    barrier = pltpu.get_barrier_semaphore()
    neighbours = (
        (lax.rem(x + 1, 4), t), (lax.rem(x + 2, 4), t), (lax.rem(x + 3, 4), t),
        (x, lax.rem(t + 1, nt)), (x, lax.rem(t + nt - 1, nt)),
    )
    for neighbour in neighbours:
        pl.semaphore_signal(barrier, inc=1, device_id=neighbour, device_id_type=MESH)

    to_below = (jnp.minimum(x + 1, 3), t)
    to_above = (jnp.maximum(x - 1, 0), t)
    to_right = (x, jnp.minimum(t + 1, nt - 1))
    to_left = (x, jnp.maximum(t - 1, 0))

    def refl_copy(l):
        return remote(reflect.at[0, l], refl_left.at[l], refl_send.at[l], refl_recv.at[l], to_right)

    def img_copy(l):
        return remote(img_out.at[l], img_in.at[l], img_send.at[l], img_recv.at[l], to_left)

    def down_copy(k):
        return remote(
            waves.at[k, slots], waves.at[k, 0], down_send.at[k], down_recv.at[k], to_below
        )

    def late_copy(k, target):
        sem = late_send.at[k, target]
        return remote(late.at[k], late_in.at[k], sem, late_recv.at[k], (target, t))

    def early_copy(k):
        return remote(early_out.at[k], early.at[k], early_send.at[k], early_recv.at[k], to_above)

    def comp_copies():
        return [
            remote(comp_out_x, comp_x, comp_send.at[0], comp_recv.at[0], to_above),
            remote(comp_out_y, comp_y, comp_send.at[1], comp_recv.at[1], to_above),
        ]

    late_in = late
    source_copies = [
        pltpu.make_async_copy(source.at[k], waves.at[k, 0], local_sem.at[5 + k])
        for k in range(shots)
    ]

    @pl.when(x == 0)
    def _():
        for copy in source_copies:
            copy.start()

    pl.semaphore_wait(barrier, 5)

    @pl.when(t < nt - 1)
    def _():
        for l in range(slots):
            refl_copy(l).start()

    j_r = lax.broadcasted_iota(jnp.int32, (width, width), 0)
    j_c = lax.broadcasted_iota(jnp.int32, (width, width), 1)
    copies[3].wait()
    for k in range(shots):
        offset = anchors[k] - (t - 1) * width
        sel_left[k] = (j_r - j_c == offset).astype(BF16)
        sel_own[k] = (j_r - j_c == offset - width).astype(BF16)
    copies[4].wait()
    level_count = counts[0]

    def live(l):
        return (level_count > l).astype(F32)

    i_r = lax.broadcasted_iota(jnp.int32, (rows, rows), 0)
    i_c = lax.broadcasted_iota(jnp.int32, (rows, rows), 1)
    eye_x = (i_r == i_c).astype(F32)
    copies[0].wait()
    for l in range(slots):
        x_re = lxv[l, 0].astype(F32)
        x_im = lxv[l, 1].astype(F32)
        if l > 0:
            x_re = x_re * live(l) + eye_x * (1.0 - live(l))
            x_im = x_im * live(l)
        xb[l, :rows, :rows] = x_re.astype(BF16)
        xb[l, :rows, rows:] = (-x_im).astype(BF16)
        xb[l, rows:, :rows] = x_im.astype(BF16)
        xb[l, rows:, rows:] = x_re.astype(BF16)
        x_ret = x_re.T
        x_imt = x_im.T
        xbt[l, :rows, :rows] = x_ret.astype(BF16)
        xbt[l, :rows, rows:] = (-x_imt).astype(BF16)
        xbt[l, rows:, :rows] = x_imt.astype(BF16)
        xbt[l, rows:, rows:] = x_ret.astype(BF16)
    copies[2].wait()
    eye_y = (j_r == j_c).astype(F32)
    for l in range(1, slots):
        yv[l, 0] = (yv[l, 0].astype(F32) * live(l) + eye_y * (1.0 - live(l))).astype(BF16)
        yv[l, 1] = (yv[l, 1].astype(F32) * live(l)).astype(BF16)
    copies[1].wait()
    for l in range(slots):
        for k in range(shots):
            win[k, l] = dot_nn(refl_own[l], sel_own[k]) * live(l)

    def finish_window(l):
        @pl.when(t > 0)
        def _():
            refl_copy(l).wait_recv()
            for k in range(shots):
                win[k, l] += dot_nn(refl_left[l], sel_left[k]) * live(l)

    def descend(k, with_windows=False):
        def level(l):
            if with_windows:
                finish_window(l)
            gain = 1.0 + win[k, l]
            scaled = jnp.concatenate(
                [
                    (gain * waves[k, l, :rows].astype(F32)).astype(BF16),
                    (gain * waves[k, l, rows:].astype(F32)).astype(BF16),
                ],
                axis=0,
            )
            middle = dot_nn(xb[l], scaled).astype(BF16)
            by_re = dot_nt(middle, yv[l, 0])
            by_im = dot_nt(middle, yv[l, 1])
            waves[k, l + 1, :rows] = (by_re[:rows] - by_im[rows:]).astype(BF16)
            waves[k, l + 1, rows:] = (by_im[:rows] + by_re[rows:]).astype(BF16)

        each_level(level)

    def each_level(level, backwards=False):
        for i in range(slots):
            level(slots - 1 - i if backwards else i)

    def ascend(wave, k, images):
        def level(l):
            back = dot_nn(xbt[l], wave[k]).astype(BF16)
            by_re = dot_nn(back, yv[l, 0])
            by_im = dot_nn(back, yv[l, 1])
            gain = win[k, l]
            d_re = waves[k, l, :rows].astype(F32)
            d_im = waves[k, l, rows:].astype(F32)
            u_re = (gain * d_re + (by_re[:rows] - by_im[rows:])).astype(BF16)
            u_im = (gain * d_im + (by_im[:rows] + by_re[rows:])).astype(BF16)
            wave[k, :rows] = u_re
            wave[k, rows:] = u_im
            if images:
                product = (d_re * u_re.astype(F32) + d_im * u_im.astype(F32)) * live(l)
                corr[k, l] = product.astype(BF16)
                if k == shots - 1:
                    finish_image(l)

        each_level(level, True)

    def finish_image(l):
        left = dot_nt(corr[0, l], sel_left[0])
        for k in range(1, shots):
            left += dot_nt(corr[k, l], sel_left[k])
        img_out[l] = left.astype(BF16)

        @pl.when(t > 0)
        def _():
            img_copy(l).start()

        own = dot_nt(corr[0, l], sel_own[0])
        for k in range(1, shots):
            own += dot_nt(corr[k, l], sel_own[k])
        out[0, l] = own

    def compose():
        own_x[...] = dot_nn(xbt[slots - 2], xbt[slots - 1]).astype(BF16)
        own_y[0], own_y[1] = yv[slots - 1, 0], yv[slots - 1, 1]
        for l in reversed(range(slots - 1)):
            if l < slots - 2:
                own_x[...] = dot_nn(xbt[l], own_x[...]).astype(BF16)
            own_y[0], own_y[1] = complex_dot(own_y[0], own_y[1], yv[l, 0], yv[l, 1])

    def carry_over(k):
        back = dot_nn(comp_x[...], late[k]).astype(BF16)
        by_re = dot_nn(back, comp_y[0])
        by_im = dot_nn(back, comp_y[1])
        held_re = early[k, :rows].astype(F32)
        held_im = early[k, rows:].astype(F32)
        late[k, :rows] = (held_re + (by_re[:rows] - by_im[rows:])).astype(BF16)
        late[k, rows:] = (held_im + (by_im[:rows] + by_re[rows:])).astype(BF16)

    @pl.when(x == 0)
    def _():
        for k in range(shots):
            source_copies[k].wait()
            descend(k, k == 0)
            down_copy(k).start()
        for copy in comp_copies():
            copy.wait_recv()
        for k in range(shots):
            early_copy(k).wait_recv()
            late_copy(k, 0).wait_recv()
            carry_over(k)
            ascend(late, k, True)

    @pl.when(x > 0)
    def _():
        for l in range(slots):
            finish_window(l)

    @pl.when(x == 1)
    def _():
        compose()
        for k in range(shots):
            down_copy(k).wait_recv()
            descend(k)
            down_copy(k).start()
        for copy in comp_copies():
            copy.wait_recv()
        comp_out_x[...] = dot_nn(own_x[...], comp_x[...]).astype(BF16)
        comp_out_y[0], comp_out_y[1] = complex_dot(comp_y[0], comp_y[1], own_y[0], own_y[1])
        for copy in comp_copies():
            copy.start()
        for k in range(shots):
            early_copy(k).wait_recv()
            early_out[k] = early[k]
            ascend(early_out, k, False)
            early_copy(k).start()
        for k in range(shots):
            late_copy(k, 1).wait_recv()
            carry_over(k)
            ascend(late, k, True)

    @pl.when(x == 2)
    def _():
        compose()
        comp_out_x[...] = own_x[...]
        comp_out_y[...] = own_y[...]
        for copy in comp_copies():
            copy.start()
        for k in range(shots):
            down_copy(k).wait_recv()
            descend(k)
            down_copy(k).start()
            early_out[k] = jnp.zeros_like(early_out[k])
            ascend(early_out, k, False)
            early_copy(k).start()
        for k in range(shots):
            late_copy(k, 2).wait_recv()
            ascend(late, k, True)

    @pl.when(x == 3)
    def _():
        for k in range(shots):
            down_copy(k).wait_recv()
            descend(k)
            late[k] = jnp.zeros_like(late[k])
            ascend(late, k, True)
            for target in (1, 0, 2):
                late_copy(k, target).start()

    @pl.when(t < nt - 1)
    def _():
        for l in reversed(range(slots)):
            img_copy(l).wait_recv()
            out[0, l] += img_in[l].astype(F32)
        for l in range(slots):
            refl_copy(l).wait_send()

    @pl.when(x < 3)
    def _():
        for k in range(shots):
            down_copy(k).wait_send()

    @pl.when((x == 1) | (x == 2))
    def _():
        for k in range(shots):
            early_copy(k).wait_send()
        for copy in comp_copies():
            copy.wait_send()

    @pl.when(x == 3)
    def _():
        for k in range(shots):
            for target in range(3):
                late_copy(k, target).wait_send()

    @pl.when(t > 0)
    def _():
        for l in range(slots):
            img_copy(l).wait_send()


def solution(mesh):
    nt = mesh.shape["tile"]

    def on_device(source, anchors, counts, reflect, lateral_x, lateral_y):
        shots, _, rows, width = source.shape
        slots = reflect.shape[1]
        any_spec = pl.BlockSpec(memory_space=pltpu.HBM)
        wave = (shots, 2 * rows, width)
        dma = pltpu.SemaphoreType.DMA
        return pl.pallas_call(
            functools.partial(kernel, nt),
            out_shape=jax.ShapeDtypeStruct((1, slots, rows, width), F32),
            in_specs=[any_spec] * 6,
            out_specs=pl.BlockSpec(memory_space=pltpu.VMEM),
            scratch_shapes=[
                pltpu.SMEM((shots,), jnp.int32),
                pltpu.SMEM((1,), jnp.int32),
                pltpu.VMEM((slots, rows, width), BF16),
                pltpu.VMEM((slots, rows, width), BF16),
                pltpu.VMEM((slots, 2, rows, rows), BF16),
                pltpu.VMEM((slots, 2, width, width), BF16),
                pltpu.VMEM((slots, 2 * rows, 2 * rows), BF16),
                pltpu.VMEM((slots, 2 * rows, 2 * rows), BF16),
                pltpu.VMEM((shots, width, width), BF16),
                pltpu.VMEM((shots, width, width), BF16),
                pltpu.VMEM((shots, slots, rows, width), F32),
                pltpu.VMEM((shots, slots + 1, 2 * rows, width), BF16),
                pltpu.VMEM(wave, BF16),
                pltpu.VMEM(wave, BF16),
                pltpu.VMEM(wave, BF16),
                pltpu.VMEM((2 * rows, 2 * rows), BF16),
                pltpu.VMEM((2, width, width), BF16),
                pltpu.VMEM((2 * rows, 2 * rows), BF16),
                pltpu.VMEM((2, width, width), BF16),
                pltpu.VMEM((2 * rows, 2 * rows), BF16),
                pltpu.VMEM((2, width, width), BF16),
                pltpu.VMEM((shots, slots, rows, width), BF16),
                pltpu.VMEM((slots, rows, width), BF16),
                pltpu.VMEM((slots, rows, width), BF16),
                dma((5 + shots,)),
                dma((slots,)), dma((slots,)),
                dma((shots,)), dma((shots,)),
                dma((shots, 3)), dma((shots,)),
                dma((shots,)), dma((shots,)),
                dma((2,)), dma((2,)),
                dma((slots,)), dma((slots,)),
            ],
            compiler_params=pltpu.CompilerParams(
                collective_id=0, has_side_effects=True, vmem_limit_bytes=64_000_000
            ),
        )(source.reshape(wave), anchors, counts, reflect, lateral_x, lateral_y)

    return jax.shard_map(
        on_device,
        mesh=mesh,
        in_specs=(
            P("tile", None, None, None),
            P("tile"),
            P("depth"),
            P("depth", None, None, "tile"),
            P("depth", None, None, None, None),
            P("depth", None, None, None, None),
        ),
        out_specs=P("depth", None, None, "tile"),
        check_vma=False,
    )
```

```python
import functools

import jax
import jax.numpy as jnp
from jax import lax
from jax.experimental import pallas as pl
from jax.experimental.pallas import tpu as pltpu
from jax.sharding import PartitionSpec as P

MESH = pl.DeviceIdType.MESH
F32 = jnp.float32
BF16 = jnp.bfloat16


def dot_nn(a, b):
    return lax.dot_general(a, b, (((1,), (0,)), ((), ())), preferred_element_type=F32)


def dot_nt(a, b):
    return lax.dot_general(a, b, (((1,), (1,)), ((), ())), preferred_element_type=F32)


def in_hbm(array):
    return pltpu.with_memory_space_constraint(array, pltpu.HBM)


def complex_dot(a_re, a_im, b_re, b_im):
    re = dot_nn(a_re, b_re) - dot_nn(a_im, b_im)
    im = dot_nn(a_re, b_im) + dot_nn(a_im, b_re)
    return re.astype(BF16), im.astype(BF16)


def kernel(
    nt,
    source, anchors_hbm, counts_hbm, reflect, lx, ly, out,
    anchors, counts, refl_own, refl_left, lxv, yv, xb, xbt, sel_own, sel_left, win,
    waves, late, early, early_out, own_x, own_y, comp_x, comp_y, comp_out_x, comp_out_y,
    corr, img_out, img_in,
    local_sem, refl_send, refl_recv, down_send, down_recv, late_send, late_recv,
    early_send, early_recv, comp_send, comp_recv, img_send, img_recv,
):
    slots, rows, width = refl_own.shape
    shots = waves.shape[0]
    x = lax.axis_index("depth")
    t = lax.axis_index("tile")

    def remote(src, dst, send, recv, target):
        return pltpu.make_async_remote_copy(
            src_ref=src, dst_ref=dst, send_sem=send, recv_sem=recv,
            device_id=target, device_id_type=MESH,
        )

    copies = [
        pltpu.make_async_copy(lx.at[0], lxv, local_sem.at[0]),
        pltpu.make_async_copy(reflect.at[0], refl_own, local_sem.at[1]),
        pltpu.make_async_copy(ly.at[0], yv, local_sem.at[2]),
        pltpu.make_async_copy(anchors_hbm, anchors, local_sem.at[3]),
        pltpu.make_async_copy(counts_hbm, counts, local_sem.at[4]),
    ]
    for copy in copies:
        copy.start()

    barrier = pltpu.get_barrier_semaphore()
    neighbours = (
        (lax.rem(x + 1, 4), t), (lax.rem(x + 2, 4), t), (lax.rem(x + 3, 4), t),
        (x, lax.rem(t + 1, nt)), (x, lax.rem(t + nt - 1, nt)),
    )
    for neighbour in neighbours:
        pl.semaphore_signal(barrier, inc=1, device_id=neighbour, device_id_type=MESH)

    to_below = (jnp.minimum(x + 1, 3), t)
    to_above = (jnp.maximum(x - 1, 0), t)
    to_right = (x, jnp.minimum(t + 1, nt - 1))
    to_left = (x, jnp.maximum(t - 1, 0))

    def refl_copy(l):
        return remote(reflect.at[0, l], refl_left.at[l], refl_send.at[l], refl_recv.at[l], to_right)

    def img_copy(l):
        return remote(img_out.at[l], img_in.at[l], img_send.at[l], img_recv.at[l], to_left)

    def down_copy(k):
        return remote(
            waves.at[k, slots], waves.at[k, 0], down_send.at[k], down_recv.at[k], to_below
        )

    def late_copy(k, target):
        sem = late_send.at[k, target]
        return remote(late.at[k], late_in.at[k], sem, late_recv.at[k], (target, t))

    def early_copy(k):
        return remote(early_out.at[k], early.at[k], early_send.at[k], early_recv.at[k], to_above)

    def comp_copies():
        return [
            remote(comp_out_x, comp_x, comp_send.at[0], comp_recv.at[0], to_above),
            remote(comp_out_y, comp_y, comp_send.at[1], comp_recv.at[1], to_above),
        ]

    late_in = late
    source_copies = [
        pltpu.make_async_copy(source.at[k], waves.at[k, 0], local_sem.at[5 + k])
        for k in range(shots)
    ]

    @pl.when(x == 0)
    def _():
        for copy in source_copies:
            copy.start()

    pl.semaphore_wait(barrier, 5)

    @pl.when(t < nt - 1)
    def _():
        for l in range(slots):
            refl_copy(l).start()

    j_r = lax.broadcasted_iota(jnp.int32, (width, width), 0)
    j_c = lax.broadcasted_iota(jnp.int32, (width, width), 1)
    copies[3].wait()
    for k in range(shots):
        offset = anchors[k] - (t - 1) * width
        sel_left[k] = (j_r - j_c == offset).astype(BF16)
        sel_own[k] = (j_r - j_c == offset - width).astype(BF16)
    copies[4].wait()
    level_count = counts[0]

    def live(l):
        return (level_count > l).astype(F32)

    i_r = lax.broadcasted_iota(jnp.int32, (rows, rows), 0)
    i_c = lax.broadcasted_iota(jnp.int32, (rows, rows), 1)
    eye_x = (i_r == i_c).astype(F32)
    copies[0].wait()
    for l in range(slots):
        x_re = lxv[l, 0].astype(F32)
        x_im = lxv[l, 1].astype(F32)
        if l > 0:
            x_re = x_re * live(l) + eye_x * (1.0 - live(l))
            x_im = x_im * live(l)
        xb[l, :rows, :rows] = x_re.astype(BF16)
        xb[l, :rows, rows:] = (-x_im).astype(BF16)
        xb[l, rows:, :rows] = x_im.astype(BF16)
        xb[l, rows:, rows:] = x_re.astype(BF16)
        x_ret = x_re.T
        x_imt = x_im.T
        xbt[l, :rows, :rows] = x_ret.astype(BF16)
        xbt[l, :rows, rows:] = (-x_imt).astype(BF16)
        xbt[l, rows:, :rows] = x_imt.astype(BF16)
        xbt[l, rows:, rows:] = x_ret.astype(BF16)
    copies[2].wait()
    eye_y = (j_r == j_c).astype(F32)
    for l in range(1, slots):
        yv[l, 0] = (yv[l, 0].astype(F32) * live(l) + eye_y * (1.0 - live(l))).astype(BF16)
        yv[l, 1] = (yv[l, 1].astype(F32) * live(l)).astype(BF16)
    copies[1].wait()
    for l in range(slots):
        for k in range(shots):
            win[k, l] = dot_nn(refl_own[l], sel_own[k]) * live(l)

    def finish_window(l):
        @pl.when(t > 0)
        def _():
            refl_copy(l).wait_recv()
            for k in range(shots):
                win[k, l] += dot_nn(refl_left[l], sel_left[k]) * live(l)

    def descend(k, with_windows=False):
        def level(l):
            if with_windows:
                finish_window(l)
            gain = 1.0 + win[k, l]
            scaled = jnp.concatenate(
                [
                    (gain * waves[k, l, :rows].astype(F32)).astype(BF16),
                    (gain * waves[k, l, rows:].astype(F32)).astype(BF16),
                ],
                axis=0,
            )
            middle = dot_nn(xb[l], scaled).astype(BF16)
            by_re = dot_nt(middle, yv[l, 0])
            by_im = dot_nt(middle, yv[l, 1])
            waves[k, l + 1, :rows] = (by_re[:rows] - by_im[rows:]).astype(BF16)
            waves[k, l + 1, rows:] = (by_im[:rows] + by_re[rows:]).astype(BF16)

        each_level(level)

    def each_level(level, backwards=False):
        for i in range(slots):
            level(slots - 1 - i if backwards else i)

    def ascend(wave, k, images):
        def level(l):
            back = dot_nn(xbt[l], wave[k]).astype(BF16)
            by_re = dot_nn(back, yv[l, 0])
            by_im = dot_nn(back, yv[l, 1])
            gain = win[k, l]
            d_re = waves[k, l, :rows].astype(F32)
            d_im = waves[k, l, rows:].astype(F32)
            u_re = (gain * d_re + (by_re[:rows] - by_im[rows:])).astype(BF16)
            u_im = (gain * d_im + (by_im[:rows] + by_re[rows:])).astype(BF16)
            wave[k, :rows] = u_re
            wave[k, rows:] = u_im
            if images:
                product = (d_re * u_re.astype(F32) + d_im * u_im.astype(F32)) * live(l)
                corr[k, l] = product.astype(BF16)
                if images == "place" and k == shots - 1:
                    finish_image(l)

        each_level(level, True)

    def finish_image(l):
        left = dot_nt(corr[0, l], sel_left[0])
        for k in range(1, shots):
            left += dot_nt(corr[k, l], sel_left[k])
        img_out[l] = left.astype(BF16)

        @pl.when(t > 0)
        def _():
            img_copy(l).start()

        own = dot_nt(corr[0, l], sel_own[0])
        for k in range(1, shots):
            own += dot_nt(corr[k, l], sel_own[k])
        out[0, l] = own

    def compose():
        own_x[...] = dot_nn(xbt[slots - 2], xbt[slots - 1]).astype(BF16)
        own_y[0], own_y[1] = yv[slots - 1, 0], yv[slots - 1, 1]
        for l in reversed(range(slots - 1)):
            if l < slots - 2:
                own_x[...] = dot_nn(xbt[l], own_x[...]).astype(BF16)
            own_y[0], own_y[1] = complex_dot(own_y[0], own_y[1], yv[l, 0], yv[l, 1])

    def carry_over(k):
        back = dot_nn(comp_x[...], late[k]).astype(BF16)
        by_re = dot_nn(back, comp_y[0])
        by_im = dot_nn(back, comp_y[1])
        held_re = early[k, :rows].astype(F32)
        held_im = early[k, rows:].astype(F32)
        late[k, :rows] = (held_re + (by_re[:rows] - by_im[rows:])).astype(BF16)
        late[k, rows:] = (held_im + (by_im[:rows] + by_re[rows:])).astype(BF16)

    @pl.when(x == 0)
    def _():
        for k in range(shots):
            source_copies[k].wait()
            descend(k, k == 0)
            down_copy(k).start()
        for copy in comp_copies():
            copy.wait_recv()
        for k in range(shots):
            early_copy(k).wait_recv()
            late_copy(k, 0).wait_recv()
            carry_over(k)
            ascend(late, k, "place")

    @pl.when(x > 0)
    def _():
        for l in range(slots):
            finish_window(l)

    @pl.when(x == 1)
    def _():
        compose()
        for k in range(shots):
            down_copy(k).wait_recv()
            descend(k)
            down_copy(k).start()
        for copy in comp_copies():
            copy.wait_recv()
        comp_out_x[...] = dot_nn(own_x[...], comp_x[...]).astype(BF16)
        comp_out_y[0], comp_out_y[1] = complex_dot(comp_y[0], comp_y[1], own_y[0], own_y[1])
        for copy in comp_copies():
            copy.start()
        for k in range(shots):
            early_copy(k).wait_recv()
            early_out[k] = early[k]
            ascend(early_out, k, False)
            early_copy(k).start()
        for k in range(shots):
            late_copy(k, 1).wait_recv()
            carry_over(k)
            ascend(late, k, "place")

    @pl.when(x == 2)
    def _():
        compose()
        comp_out_x[...] = own_x[...]
        comp_out_y[...] = own_y[...]
        for copy in comp_copies():
            copy.start()
        for k in range(shots):
            down_copy(k).wait_recv()
            descend(k)
            down_copy(k).start()
            early_out[k] = jnp.zeros_like(early_out[k])
            ascend(early_out, k, False)
            early_copy(k).start()
        for k in range(shots):
            late_copy(k, 2).wait_recv()
            ascend(late, k, "place")

    @pl.when(x == 3)
    def _():
        for k in range(shots):
            down_copy(k).wait_recv()
            descend(k)
            late[k] = jnp.zeros_like(late[k])
            ascend(late, k, True)
            for target in (1, 0, 2):
                late_copy(k, target).start()
        for l in range(slots):
            finish_image(l)

    @pl.when(t < nt - 1)
    def _():
        for l in reversed(range(slots)):
            img_copy(l).wait_recv()
            out[0, l] += img_in[l].astype(F32)
        for l in range(slots):
            refl_copy(l).wait_send()

    @pl.when(x < 3)
    def _():
        for k in range(shots):
            down_copy(k).wait_send()

    @pl.when((x == 1) | (x == 2))
    def _():
        for k in range(shots):
            early_copy(k).wait_send()
        for copy in comp_copies():
            copy.wait_send()

    @pl.when(x == 3)
    def _():
        for k in range(shots):
            for target in range(3):
                late_copy(k, target).wait_send()

    @pl.when(t > 0)
    def _():
        for l in range(slots):
            img_copy(l).wait_send()


def solution(mesh):
    nt = mesh.shape["tile"]

    def on_device(source, anchors, counts, reflect, lateral_x, lateral_y):
        shots, _, rows, width = source.shape
        slots = reflect.shape[1]
        any_spec = pl.BlockSpec(memory_space=pltpu.HBM)
        wave = (shots, 2 * rows, width)
        dma = pltpu.SemaphoreType.DMA
        return pl.pallas_call(
            functools.partial(kernel, nt),
            out_shape=jax.ShapeDtypeStruct((1, slots, rows, width), F32),
            in_specs=[any_spec] * 6,
            out_specs=pl.BlockSpec(memory_space=pltpu.VMEM),
            scratch_shapes=[
                pltpu.SMEM((shots,), jnp.int32),
                pltpu.SMEM((1,), jnp.int32),
                pltpu.VMEM((slots, rows, width), BF16),
                pltpu.VMEM((slots, rows, width), BF16),
                pltpu.VMEM((slots, 2, rows, rows), BF16),
                pltpu.VMEM((slots, 2, width, width), BF16),
                pltpu.VMEM((slots, 2 * rows, 2 * rows), BF16),
                pltpu.VMEM((slots, 2 * rows, 2 * rows), BF16),
                pltpu.VMEM((shots, width, width), BF16),
                pltpu.VMEM((shots, width, width), BF16),
                pltpu.VMEM((shots, slots, rows, width), F32),
                pltpu.VMEM((shots, slots + 1, 2 * rows, width), BF16),
                pltpu.VMEM(wave, BF16),
                pltpu.VMEM(wave, BF16),
                pltpu.VMEM(wave, BF16),
                pltpu.VMEM((2 * rows, 2 * rows), BF16),
                pltpu.VMEM((2, width, width), BF16),
                pltpu.VMEM((2 * rows, 2 * rows), BF16),
                pltpu.VMEM((2, width, width), BF16),
                pltpu.VMEM((2 * rows, 2 * rows), BF16),
                pltpu.VMEM((2, width, width), BF16),
                pltpu.VMEM((shots, slots, rows, width), BF16),
                pltpu.VMEM((slots, rows, width), BF16),
                pltpu.VMEM((slots, rows, width), BF16),
                dma((5 + shots,)),
                dma((slots,)), dma((slots,)),
                dma((shots,)), dma((shots,)),
                dma((shots, 3)), dma((shots,)),
                dma((shots,)), dma((shots,)),
                dma((2,)), dma((2,)),
                dma((slots,)), dma((slots,)),
            ],
            compiler_params=pltpu.CompilerParams(
                collective_id=0, has_side_effects=True, vmem_limit_bytes=16 * 1024 * 1024
            ),
        )(in_hbm(source.reshape(wave)), in_hbm(anchors), counts, in_hbm(reflect), in_hbm(lateral_x), in_hbm(lateral_y))

    return jax.shard_map(
        on_device,
        mesh=mesh,
        in_specs=(
            P("tile", None, None, None),
            P("tile"),
            P("depth"),
            P("depth", None, None, "tile"),
            P("depth", None, None, None, None),
            P("depth", None, None, None, None),
        ),
        out_specs=P("depth", None, None, "tile"),
        check_vma=False,
    )
```

```python
import functools

import jax
import jax.numpy as jnp
from jax import lax
from jax.experimental import pallas as pl
from jax.experimental.pallas import tpu as pltpu
from jax.sharding import PartitionSpec as P

MESH = pl.DeviceIdType.MESH
F32 = jnp.float32
BF16 = jnp.bfloat16


def dot_nn(a, b):
    return lax.dot_general(a, b, (((1,), (0,)), ((), ())), preferred_element_type=F32)


def dot_nt(a, b):
    return lax.dot_general(a, b, (((1,), (1,)), ((), ())), preferred_element_type=F32)


def in_hbm(array):
    return pltpu.with_memory_space_constraint(array, pltpu.HBM)


def complex_dot(a_re, a_im, b_re, b_im):
    re = dot_nn(a_re, b_re) - dot_nn(a_im, b_im)
    im = dot_nn(a_re, b_im) + dot_nn(a_im, b_re)
    return re.astype(BF16), im.astype(BF16)


def kernel(
    nt,
    source, anchors_hbm, counts_hbm, reflect, lx, ly, out,
    anchors, counts, refl_own, refl_left, lxv, yv, xb, xbt, sel_own, sel_left, win,
    waves, late, early, early_out, own_x, own_y, comp_x, comp_y, both_x, both_y,
    near_x, near_y, kept, left_acc, corr, img_out, img_in,
    local_sem, refl_send, refl_recv, down_send, down_recv, late_send, late_recv,
    early_send, early_recv, comp_send, comp_recv, near_send, near_recv,
    img_send, img_recv,
):
    slots, rows, width = refl_own.shape
    shots = waves.shape[0]
    x = lax.axis_index("depth")
    t = lax.axis_index("tile")

    def remote(src, dst, send, recv, target):
        return pltpu.make_async_remote_copy(
            src_ref=src, dst_ref=dst, send_sem=send, recv_sem=recv,
            device_id=target, device_id_type=MESH,
        )

    copies = [
        pltpu.make_async_copy(lx.at[0], lxv, local_sem.at[0]),
        pltpu.make_async_copy(reflect.at[0], refl_own, local_sem.at[1]),
        pltpu.make_async_copy(ly.at[0], yv, local_sem.at[2]),
        pltpu.make_async_copy(anchors_hbm, anchors, local_sem.at[3]),
        pltpu.make_async_copy(counts_hbm, counts, local_sem.at[4]),
    ]
    for i in (1, 3, 4, 0, 2):
        copies[i].start()

    barrier = pltpu.get_barrier_semaphore()
    neighbours = (
        (lax.rem(x + 2, 4), t), (x, lax.rem(t + 1, nt)), (x, lax.rem(t + nt - 1, nt)),
        (lax.rem(x + 1, 4), t), (lax.rem(x + 3, 4), t),
    )
    for neighbour in neighbours:
        pl.semaphore_signal(barrier, inc=1, device_id=neighbour, device_id_type=MESH)

    to_below = (jnp.minimum(x + 1, 3), t)
    to_above = (jnp.maximum(x - 1, 0), t)
    to_right = (x, jnp.minimum(t + 1, nt - 1))
    to_left = (x, jnp.maximum(t - 1, 0))

    def refl_copy(l):
        return remote(refl_own.at[l], refl_left.at[l], refl_send.at[l], refl_recv.at[l], to_right)

    def img_copy(l):
        return remote(img_out.at[l], img_in.at[l], img_send.at[l], img_recv.at[l], to_left)

    def down_copy(k):
        return remote(
            waves.at[k, slots], waves.at[k, 0], down_send.at[k], down_recv.at[k], to_below
        )

    def late_copy(k, target):
        sem = late_send.at[k, target]
        return remote(late.at[k], late_in.at[k], sem, late_recv.at[k], (target, t))

    def early_copy(k):
        return remote(early_out.at[k], early.at[k], early_send.at[k], early_recv.at[k], to_above)

    def comp_copies(target):
        return [
            remote(own_x, comp_x, comp_send.at[0, target], comp_recv.at[0], (target, t)),
            remote(own_y, comp_y, comp_send.at[1, target], comp_recv.at[1], (target, t)),
        ]

    def near_copies():
        return [
            remote(own_x, near_x, near_send.at[0], near_recv.at[0], to_above),
            remote(own_y, near_y, near_send.at[1], near_recv.at[1], to_above),
        ]

    late_in = late
    source_copies = [
        pltpu.make_async_copy(source.at[k], waves.at[k, 0], local_sem.at[5 + k])
        for k in range(shots)
    ]

    @pl.when(x == 0)
    def _():
        for copy in source_copies:
            copy.start()

    copies[1].wait()
    pl.semaphore_wait(barrier, 5)

    @pl.when(t < nt - 1)
    def _():
        for l in range(slots):
            refl_copy(l).start()

    j_r = lax.broadcasted_iota(jnp.int32, (width, width), 0)
    j_c = lax.broadcasted_iota(jnp.int32, (width, width), 1)
    copies[3].wait()
    for k in range(shots):
        offset = anchors[k] - (t - 1) * width
        sel_left[k] = (j_r - j_c == offset).astype(BF16)
        sel_own[k] = (j_r - j_c == offset - width).astype(BF16)
    copies[4].wait()
    level_count = counts[0]

    def live(l):
        return (level_count > l).astype(F32)

    i_r = lax.broadcasted_iota(jnp.int32, (rows, rows), 0)
    i_c = lax.broadcasted_iota(jnp.int32, (rows, rows), 1)
    eye_x = (i_r == i_c).astype(F32)
    copies[0].wait()
    for l in range(slots):
        x_re = lxv[l, 0].astype(F32)
        x_im = lxv[l, 1].astype(F32)
        if l > 0:
            x_re = x_re * live(l) + eye_x * (1.0 - live(l))
            x_im = x_im * live(l)
        xb[l, :rows, :rows] = x_re.astype(BF16)
        xb[l, :rows, rows:] = (-x_im).astype(BF16)
        xb[l, rows:, :rows] = x_im.astype(BF16)
        xb[l, rows:, rows:] = x_re.astype(BF16)
        x_ret = x_re.T
        x_imt = x_im.T
        xbt[l, :rows, :rows] = x_ret.astype(BF16)
        xbt[l, :rows, rows:] = (-x_imt).astype(BF16)
        xbt[l, rows:, :rows] = x_imt.astype(BF16)
        xbt[l, rows:, rows:] = x_ret.astype(BF16)
    copies[2].wait()
    eye_y = (j_r == j_c).astype(F32)
    for l in range(1, slots):
        yv[l, 0] = (yv[l, 0].astype(F32) * live(l) + eye_y * (1.0 - live(l))).astype(BF16)
        yv[l, 1] = (yv[l, 1].astype(F32) * live(l)).astype(BF16)
    for l in range(slots):
        for k in range(shots):
            win[k, l] = dot_nn(refl_own[l], sel_own[k]) * live(l)

    def finish_window(l, first_shot=True, others=True):
        @pl.when(t > 0)
        def _():
            if first_shot:
                refl_copy(l).wait_recv()
                win[0, l] += dot_nn(refl_left[l], sel_left[0]) * live(l)
            if others:
                for k in range(1, shots):
                    win[k, l] += dot_nn(refl_left[l], sel_left[k]) * live(l)

    def descend(k, with_windows=False, steps=slots):
        def level(l):
            if with_windows:
                finish_window(l, k == 0, k == 1)
            gain = 1.0 + win[k, l]
            scaled = jnp.concatenate(
                [
                    (gain * waves[k, l, :rows].astype(F32)).astype(BF16),
                    (gain * waves[k, l, rows:].astype(F32)).astype(BF16),
                ],
                axis=0,
            )
            middle = dot_nn(xb[l], scaled).astype(BF16)
            by_re = dot_nt(middle, yv[l, 0])
            by_im = dot_nt(middle, yv[l, 1])
            waves[k, l + 1, :rows] = (by_re[:rows] - by_im[rows:]).astype(BF16)
            waves[k, l + 1, rows:] = (by_im[:rows] + by_re[rows:]).astype(BF16)

        for l in range(steps):
            level(l)

    def ascend(wave, k, images=None, from_zero=False, last=False):
        def level(l):
            gain = win[k, l]
            d_re = waves[k, l, :rows].astype(F32)
            d_im = waves[k, l, rows:].astype(F32)
            if from_zero and l == slots - 1:
                u_re = (gain * d_re).astype(BF16)
                u_im = (gain * d_im).astype(BF16)
            else:
                back = dot_nn(xbt[l], wave[k]).astype(BF16)
                by_re = dot_nn(back, yv[l, 0])
                by_im = dot_nn(back, yv[l, 1])
                u_re = (gain * d_re + (by_re[:rows] - by_im[rows:])).astype(BF16)
                u_im = (gain * d_im + (by_im[:rows] + by_re[rows:])).astype(BF16)
            wave[k, :rows] = u_re
            wave[k, rows:] = u_im
            if images == "keep":
                kept[k, l, :rows] = u_re
                kept[k, l, rows:] = u_im
            if images == "place":
                product = (d_re * u_re.astype(F32) + d_im * u_im.astype(F32)) * live(l)
                corr[k, l] = product.astype(BF16)
                if last:
                    image_left(l, k)

        for l in reversed(range(slots)):
            level(l)
        if images == "place":
            for l in reversed(range(slots)):
                if last:
                    image_own(l, k)
                else:
                    image_first(l, k)

    def image_first(l, k):
        left_acc[l] = dot_nt(corr[k, l], sel_left[k])
        out[0, l] = dot_nt(corr[k, l], sel_own[k])

    def image_left(l, k):
        img_out[l] = (left_acc[l] + dot_nt(corr[k, l], sel_left[k])).astype(BF16)

        @pl.when(t > 0)
        def _():
            img_copy(l).start()

    def image_own(l, k):
        out[0, l] += dot_nt(corr[k, l], sel_own[k])

    def compose():
        own_x[...] = dot_nn(xbt[slots - 2], xbt[slots - 1]).astype(BF16)
        own_y[0], own_y[1] = yv[slots - 1, 0], yv[slots - 1, 1]
        for l in reversed(range(slots - 1)):
            if l < slots - 2:
                own_x[...] = dot_nn(xbt[l], own_x[...]).astype(BF16)
            own_y[0], own_y[1] = complex_dot(own_y[0], own_y[1], yv[l, 0], yv[l, 1])

    def carry_over(op_x, op_y, wave, held, k, into):
        back = dot_nn(op_x[...], wave[k]).astype(BF16)
        by_re = dot_nn(back, op_y[0])
        by_im = dot_nn(back, op_y[1])
        held_re = held[k, :rows].astype(F32)
        held_im = held[k, rows:].astype(F32)
        into[k, :rows] = (held_re + (by_re[:rows] - by_im[rows:])).astype(BF16)
        into[k, rows:] = (held_im + (by_im[:rows] + by_re[rows:])).astype(BF16)

    @pl.when(x == 0)
    def _():
        for k in range(shots):
            source_copies[k].wait()
            descend(k, True)
            down_copy(k).start()
        for copy in near_copies() + comp_copies(0):
            copy.wait_recv()
        both_x[...] = dot_nn(near_x[...], comp_x[...]).astype(BF16)
        both_y[0], both_y[1] = complex_dot(comp_y[0], comp_y[1], near_y[0], near_y[1])
        for k in range(shots):
            early_copy(k).wait_recv()
            late_copy(k, 0).wait_recv()
            carry_over(both_x, both_y, late, early, k, late)
            ascend(late, k, "place", last=k == 1)

    @pl.when(x > 0)
    def _():
        for l in range(slots):
            finish_window(l)

    @pl.when(x == 1)
    def _():
        compose()
        for copy in near_copies():
            copy.start()
        for k in range(shots):
            down_copy(k).wait_recv()
            descend(k)
            down_copy(k).start()
        for k in range(shots):
            ascend(early_out, k, from_zero=True)
        for k in range(shots):
            early_copy(k).wait_recv()
            carry_over(own_x, own_y, early, early_out, k, early_out)
            early_copy(k).start()
        for copy in comp_copies(1):
            copy.wait_recv()
        for k in reversed(range(shots)):
            late_copy(k, 1).wait_recv()
            carry_over(comp_x, comp_y, late, early, k, late)
            ascend(late, k, "place", last=k == 0)

    @pl.when(x == 2)
    def _():
        compose()
        for copy in comp_copies(1) + comp_copies(0):
            copy.start()
        for k in range(shots):
            down_copy(k).wait_recv()
            descend(k)
            down_copy(k).start()
            ascend(early_out, k, from_zero=True)
            early_copy(k).start()
        late_copy(0, 2).wait_recv()
        late_copy(0, 1).start()
        early[0] = late[0]
        ascend(early, 0, "place")
        late_copy(1, 2).wait_recv()
        ascend(late, 1, "place", last=True)

    @pl.when(x == 3)
    def _():
        for k in range(shots):
            down_copy(k).wait_recv()
            descend(k, steps=slots - 1)
            ascend(late, k, "keep", from_zero=True)
            for target in ((0, 2), (1, 0))[k]:
                late_copy(k, target).start()
        late_copy(1, 1).wait_send()
        late_copy(1, 2).start()
        for l in reversed(range(slots)):
            for k in range(shots):
                product = waves[k, l].astype(F32) * kept[k, l].astype(F32)
                corr[k, l] = ((product[:rows] + product[rows:]) * live(l)).astype(BF16)
            image_first(l, 0)
            image_left(l, 1)
            image_own(l, 1)

    @pl.when(t < nt - 1)
    def _():
        for l in reversed(range(slots)):
            img_copy(l).wait_recv()
            out[0, l] += img_in[l].astype(F32)
        for l in range(slots):
            refl_copy(l).wait_send()

    @pl.when(x < 3)
    def _():
        for k in range(shots):
            down_copy(k).wait_send()

    @pl.when((x == 1) | (x == 2))
    def _():
        for k in range(shots):
            early_copy(k).wait_send()
    @pl.when(x == 1)
    def _():
        for copy in near_copies():
            copy.wait_send()

    @pl.when(x == 2)
    def _():
        for copy in comp_copies(1) + comp_copies(0):
            copy.wait_send()

    @pl.when(x == 3)
    def _():
        for k, target in ((0, 0), (0, 2), (1, 0), (1, 2)):
            late_copy(k, target).wait_send()

    @pl.when(x == 2)
    def _():
        late_copy(0, 1).wait_send()

    @pl.when(t > 0)
    def _():
        for l in range(slots):
            img_copy(l).wait_send()


def solution(mesh):
    nt = mesh.shape["tile"]

    def on_device(source, anchors, counts, reflect, lateral_x, lateral_y):
        shots, _, rows, width = source.shape
        slots = reflect.shape[1]
        any_spec = pl.BlockSpec(memory_space=pltpu.HBM)
        wave = (shots, 2 * rows, width)
        dma = pltpu.SemaphoreType.DMA
        return pl.pallas_call(
            functools.partial(kernel, nt),
            out_shape=jax.ShapeDtypeStruct((1, slots, rows, width), F32),
            in_specs=[any_spec] * 6,
            out_specs=pl.BlockSpec(memory_space=pltpu.VMEM),
            scratch_shapes=[
                pltpu.SMEM((shots,), jnp.int32),
                pltpu.SMEM((1,), jnp.int32),
                pltpu.VMEM((slots, rows, width), BF16),
                pltpu.VMEM((slots, rows, width), BF16),
                pltpu.VMEM((slots, 2, rows, rows), BF16),
                pltpu.VMEM((slots, 2, width, width), BF16),
                pltpu.VMEM((slots, 2 * rows, 2 * rows), BF16),
                pltpu.VMEM((slots, 2 * rows, 2 * rows), BF16),
                pltpu.VMEM((shots, width, width), BF16),
                pltpu.VMEM((shots, width, width), BF16),
                pltpu.VMEM((shots, slots, rows, width), F32),
                pltpu.VMEM((shots, slots + 1, 2 * rows, width), BF16),
                pltpu.VMEM(wave, BF16),
                pltpu.VMEM(wave, BF16),
                pltpu.VMEM(wave, BF16),
                pltpu.VMEM((2 * rows, 2 * rows), BF16),
                pltpu.VMEM((2, width, width), BF16),
                pltpu.VMEM((2 * rows, 2 * rows), BF16),
                pltpu.VMEM((2, width, width), BF16),
                pltpu.VMEM((2 * rows, 2 * rows), BF16),
                pltpu.VMEM((2, width, width), BF16),
                pltpu.VMEM((2 * rows, 2 * rows), BF16),
                pltpu.VMEM((2, width, width), BF16),
                pltpu.VMEM((shots, slots, 2 * rows, width), BF16),
                pltpu.VMEM((slots, rows, width), F32),
                pltpu.VMEM((shots, slots, rows, width), BF16),
                pltpu.VMEM((slots, rows, width), BF16),
                pltpu.VMEM((slots, rows, width), BF16),
                dma((5 + shots,)),
                dma((slots,)), dma((slots,)),
                dma((shots,)), dma((shots,)),
                dma((shots, 3)), dma((shots,)),
                dma((shots,)), dma((shots,)),
                dma((2, 2)), dma((2,)),
                dma((2,)), dma((2,)),
                dma((slots,)), dma((slots,)),
            ],
            compiler_params=pltpu.CompilerParams(
                collective_id=0, has_side_effects=True, vmem_limit_bytes=16 * 1024 * 1024
            ),
        )(in_hbm(source.reshape(wave)), in_hbm(anchors), counts, in_hbm(reflect), in_hbm(lateral_x), in_hbm(lateral_y))

    return jax.shard_map(
        on_device,
        mesh=mesh,
        in_specs=(
            P("tile", None, None, None),
            P("tile"),
            P("depth"),
            P("depth", None, None, "tile"),
            P("depth", None, None, None, None),
            P("depth", None, None, None, None),
        ),
        out_specs=P("depth", None, None, "tile"),
        check_vma=False,
    )
```

```python
import functools

import jax
import jax.numpy as jnp
from jax import lax
from jax.experimental import pallas as pl
from jax.experimental.pallas import tpu as pltpu
from jax.sharding import PartitionSpec as P

MESH = pl.DeviceIdType.MESH
F32 = jnp.float32
BF16 = jnp.bfloat16


def dot_nn(a, b):
    return lax.dot_general(a, b, (((1,), (0,)), ((), ())), preferred_element_type=F32)


def dot_nt(a, b):
    return lax.dot_general(a, b, (((1,), (1,)), ((), ())), preferred_element_type=F32)


def in_hbm(array):
    return pltpu.with_memory_space_constraint(array, pltpu.HBM)


def complex_dot(a_re, a_im, b_re, b_im):
    re = dot_nn(a_re, b_re) - dot_nn(a_im, b_im)
    im = dot_nn(a_re, b_im) + dot_nn(a_im, b_re)
    return re.astype(BF16), im.astype(BF16)


def kernel(
    nt,
    source, anchors_hbm, counts_hbm, reflect, lx, ly, out,
    anchors, counts, refl_own, refl_left, lxv, yv, xb, xbt, sel_own, sel_left, win,
    waves, late, early, early_out, own_x, own_y, comp_x, comp_y, both_x, both_y,
    near_x, near_y, kept, left_acc, corr, img_out, img_in,
    local_sem, refl_send, refl_recv, down_send, down_recv, late_send, late_recv,
    early_send, early_recv, comp_send, comp_recv, near_send, near_recv,
    img_send, img_recv,
):
    slots, rows, width = refl_own.shape
    shots = waves.shape[0]
    x = lax.axis_index("depth")
    t = lax.axis_index("tile")

    def remote(src, dst, send, recv, target):
        return pltpu.make_async_remote_copy(
            src_ref=src, dst_ref=dst, send_sem=send, recv_sem=recv,
            device_id=target, device_id_type=MESH,
        )

    copies = [
        pltpu.make_async_copy(lx.at[0], lxv, local_sem.at[0]),
        pltpu.make_async_copy(reflect.at[0], refl_own, local_sem.at[1]),
        pltpu.make_async_copy(ly.at[0], yv, local_sem.at[2]),
        pltpu.make_async_copy(anchors_hbm, anchors, local_sem.at[3]),
        pltpu.make_async_copy(counts_hbm, counts, local_sem.at[4]),
    ]
    for i in (1, 3, 4, 0, 2):
        copies[i].start()

    barrier = pltpu.get_barrier_semaphore()
    neighbours = (
        (lax.rem(x + 2, 4), t), (x, lax.rem(t + 1, nt)), (x, lax.rem(t + nt - 1, nt)),
        (lax.rem(x + 1, 4), t), (lax.rem(x + 3, 4), t),
    )
    for neighbour in neighbours:
        pl.semaphore_signal(barrier, inc=1, device_id=neighbour, device_id_type=MESH)

    to_below = (jnp.minimum(x + 1, 3), t)
    to_above = (jnp.maximum(x - 1, 0), t)
    to_right = (x, jnp.minimum(t + 1, nt - 1))
    to_left = (x, jnp.maximum(t - 1, 0))

    def refl_copy(l):
        return remote(refl_own.at[l], refl_left.at[l], refl_send.at[l], refl_recv.at[l], to_right)

    def img_copy(l):
        return remote(img_out.at[l], img_in.at[l], img_send.at[l], img_recv.at[l], to_left)

    def down_copy(k):
        return remote(
            waves.at[k, slots], waves.at[k, 0], down_send.at[k], down_recv.at[k], to_below
        )

    def late_copy(k, target):
        sem = late_send.at[k, target]
        return remote(late.at[k], late_in.at[k], sem, late_recv.at[k], (target, t))

    def early_copy(k):
        return remote(early_out.at[k], early.at[k], early_send.at[k], early_recv.at[k], to_above)

    def comp_copies(target):
        return [
            remote(own_x, comp_x, comp_send.at[0, target], comp_recv.at[0], (target, t)),
            remote(own_y, comp_y, comp_send.at[1, target], comp_recv.at[1], (target, t)),
        ]

    def near_copies():
        return [
            remote(own_x, near_x, near_send.at[0], near_recv.at[0], to_above),
            remote(own_y, near_y, near_send.at[1], near_recv.at[1], to_above),
        ]

    late_in = late
    source_copies = [
        pltpu.make_async_copy(source.at[k], waves.at[k, 0], local_sem.at[5 + k])
        for k in range(shots)
    ]

    @pl.when(x == 0)
    def _():
        for copy in source_copies:
            copy.start()

    copies[1].wait()
    pl.semaphore_wait(barrier, 5)

    @pl.when(t < nt - 1)
    def _():
        for l in range(slots):
            refl_copy(l).start()

    j_r = lax.broadcasted_iota(jnp.int32, (width, width), 0)
    j_c = lax.broadcasted_iota(jnp.int32, (width, width), 1)
    copies[3].wait()
    for k in range(shots):
        offset = anchors[k] - (t - 1) * width
        sel_left[k] = (j_r - j_c == offset).astype(BF16)
        sel_own[k] = (j_r - j_c == offset - width).astype(BF16)
    copies[4].wait()
    level_count = counts[0]

    def live(l):
        return (level_count > l).astype(F32)

    i_r = lax.broadcasted_iota(jnp.int32, (rows, rows), 0)
    i_c = lax.broadcasted_iota(jnp.int32, (rows, rows), 1)
    eye_x = (i_r == i_c).astype(F32)
    copies[0].wait()
    for l in range(slots):
        x_re = lxv[l, 0].astype(F32)
        x_im = lxv[l, 1].astype(F32)
        if l > 0:
            x_re = x_re * live(l) + eye_x * (1.0 - live(l))
            x_im = x_im * live(l)
        xb[l, :rows, :rows] = x_re.astype(BF16)
        xb[l, :rows, rows:] = (-x_im).astype(BF16)
        xb[l, rows:, :rows] = x_im.astype(BF16)
        xb[l, rows:, rows:] = x_re.astype(BF16)

    def transpose_operators():
        for l in range(slots):
            x_ret = xb[l, :rows, :rows].astype(F32).T
            x_imt = xb[l, rows:, :rows].astype(F32).T
            xbt[l, :rows, :rows] = x_ret.astype(BF16)
            xbt[l, :rows, rows:] = (-x_imt).astype(BF16)
            xbt[l, rows:, :rows] = x_imt.astype(BF16)
            xbt[l, rows:, rows:] = x_ret.astype(BF16)

    copies[2].wait()
    eye_y = (j_r == j_c).astype(F32)
    for l in range(1, slots):
        yv[l, 0] = (yv[l, 0].astype(F32) * live(l) + eye_y * (1.0 - live(l))).astype(BF16)
        yv[l, 1] = (yv[l, 1].astype(F32) * live(l)).astype(BF16)
    for l in range(slots):
        for k in range(shots):
            win[k, l] = dot_nn(refl_own[l], sel_own[k]) * live(l)

    def finish_window(l, first_shot=True, others=True):
        @pl.when(t > 0)
        def _():
            if first_shot:
                refl_copy(l).wait_recv()
                win[0, l] += dot_nn(refl_left[l], sel_left[0]) * live(l)
            if others:
                for k in range(1, shots):
                    win[k, l] += dot_nn(refl_left[l], sel_left[k]) * live(l)

    def descend(k, with_windows=False, steps=slots):
        def level(l):
            if with_windows:
                finish_window(l, k == 0, k == 1)
            gain = 1.0 + win[k, l]
            scaled = jnp.concatenate(
                [
                    (gain * waves[k, l, :rows].astype(F32)).astype(BF16),
                    (gain * waves[k, l, rows:].astype(F32)).astype(BF16),
                ],
                axis=0,
            )
            middle = dot_nn(xb[l], scaled).astype(BF16)
            by_re = dot_nt(middle, yv[l, 0])
            by_im = dot_nt(middle, yv[l, 1])
            waves[k, l + 1, :rows] = (by_re[:rows] - by_im[rows:]).astype(BF16)
            waves[k, l + 1, rows:] = (by_im[:rows] + by_re[rows:]).astype(BF16)

        for l in range(steps):
            level(l)

    def ascend(wave, k, images=None, from_zero=False, last=False):
        def level(l):
            gain = win[k, l]
            d_re = waves[k, l, :rows].astype(F32)
            d_im = waves[k, l, rows:].astype(F32)
            if from_zero and l == slots - 1:
                u_re = (gain * d_re).astype(BF16)
                u_im = (gain * d_im).astype(BF16)
            else:
                back = dot_nn(xbt[l], wave[k]).astype(BF16)
                by_re = dot_nn(back, yv[l, 0])
                by_im = dot_nn(back, yv[l, 1])
                u_re = (gain * d_re + (by_re[:rows] - by_im[rows:])).astype(BF16)
                u_im = (gain * d_im + (by_im[:rows] + by_re[rows:])).astype(BF16)
            wave[k, :rows] = u_re
            wave[k, rows:] = u_im
            if images == "keep":
                kept[k, l, :rows] = u_re
                kept[k, l, rows:] = u_im
            if images == "place":
                product = (d_re * u_re.astype(F32) + d_im * u_im.astype(F32)) * live(l)
                corr[k, l] = product.astype(BF16)
                if last:
                    image_left(l, k)

        for l in reversed(range(slots)):
            level(l)
        if images == "place":
            for l in reversed(range(slots)):
                if last:
                    image_own(l, k)
                else:
                    image_first(l, k)

    def image_first(l, k):
        left_acc[l] = dot_nt(corr[k, l], sel_left[k])
        out[0, l] = dot_nt(corr[k, l], sel_own[k])

    def image_left(l, k):
        img_out[l] = (left_acc[l] + dot_nt(corr[k, l], sel_left[k])).astype(BF16)

        @pl.when(t > 0)
        def _():
            img_copy(l).start()

    def image_own(l, k):
        out[0, l] += dot_nt(corr[k, l], sel_own[k])

    def compose():
        own_x[...] = dot_nn(xbt[slots - 2], xbt[slots - 1]).astype(BF16)
        own_y[0], own_y[1] = yv[slots - 1, 0], yv[slots - 1, 1]
        for l in reversed(range(slots - 1)):
            if l < slots - 2:
                own_x[...] = dot_nn(xbt[l], own_x[...]).astype(BF16)
            own_y[0], own_y[1] = complex_dot(own_y[0], own_y[1], yv[l, 0], yv[l, 1])

    def carry_over(op_x, op_y, wave, held, k, into):
        back = dot_nn(op_x[...], wave[k]).astype(BF16)
        by_re = dot_nn(back, op_y[0])
        by_im = dot_nn(back, op_y[1])
        held_re = held[k, :rows].astype(F32)
        held_im = held[k, rows:].astype(F32)
        into[k, :rows] = (held_re + (by_re[:rows] - by_im[rows:])).astype(BF16)
        into[k, rows:] = (held_im + (by_im[:rows] + by_re[rows:])).astype(BF16)

    @pl.when(x == 0)
    def _():
        for k in range(shots):
            source_copies[k].wait()
            descend(k, True)
            down_copy(k).start()
        transpose_operators()
        for copy in near_copies() + comp_copies(0):
            copy.wait_recv()
        both_x[...] = dot_nn(near_x[...], comp_x[...]).astype(BF16)
        both_y[0], both_y[1] = complex_dot(comp_y[0], comp_y[1], near_y[0], near_y[1])
        for k in range(shots):
            early_copy(k).wait_recv()
            late_copy(k, 0).wait_recv()
            carry_over(both_x, both_y, late, early, k, late)
            ascend(late, k, "place", last=k == 1)

    @pl.when(x > 0)
    def _():
        transpose_operators()
        for l in range(slots):
            finish_window(l)

    @pl.when(x == 1)
    def _():
        compose()
        for copy in near_copies():
            copy.start()
        for k in range(shots):
            down_copy(k).wait_recv()
            descend(k)
            down_copy(k).start()
        for k in range(shots):
            ascend(early_out, k, from_zero=True)
        for k in range(shots):
            early_copy(k).wait_recv()
            carry_over(own_x, own_y, early, early_out, k, early_out)
            early_copy(k).start()
        for copy in comp_copies(1):
            copy.wait_recv()
        for k in reversed(range(shots)):
            late_copy(k, 1).wait_recv()
            carry_over(comp_x, comp_y, late, early, k, late)
            ascend(late, k, "place", last=k == 0)

    @pl.when(x == 2)
    def _():
        compose()
        for copy in comp_copies(1) + comp_copies(0):
            copy.start()
        for k in range(shots):
            down_copy(k).wait_recv()
            descend(k)
            down_copy(k).start()
            ascend(early_out, k, from_zero=True)
            early_copy(k).start()
        late_copy(0, 2).wait_recv()
        late_copy(0, 1).start()
        early[0] = late[0]
        ascend(early, 0, "place")
        late_copy(1, 2).wait_recv()
        ascend(late, 1, "place", last=True)

    @pl.when(x == 3)
    def _():
        for k in range(shots):
            down_copy(k).wait_recv()
            descend(k, steps=slots - 1)
            ascend(late, k, "keep", from_zero=True)
            for target in ((0, 2), (1, 0))[k]:
                late_copy(k, target).start()
        late_copy(1, 1).wait_send()
        late_copy(1, 2).start()
        for l in reversed(range(slots)):
            for k in range(shots):
                product = waves[k, l].astype(F32) * kept[k, l].astype(F32)
                corr[k, l] = ((product[:rows] + product[rows:]) * live(l)).astype(BF16)
            image_first(l, 0)
            image_left(l, 1)
            image_own(l, 1)

    @pl.when(t < nt - 1)
    def _():
        for l in reversed(range(slots)):
            img_copy(l).wait_recv()
            out[0, l] += img_in[l].astype(F32)
        for l in range(slots):
            refl_copy(l).wait_send()

    @pl.when(x < 3)
    def _():
        for k in range(shots):
            down_copy(k).wait_send()

    @pl.when((x == 1) | (x == 2))
    def _():
        for k in range(shots):
            early_copy(k).wait_send()
    @pl.when(x == 1)
    def _():
        for copy in near_copies():
            copy.wait_send()

    @pl.when(x == 2)
    def _():
        for copy in comp_copies(1) + comp_copies(0):
            copy.wait_send()

    @pl.when(x == 3)
    def _():
        for k, target in ((0, 0), (0, 2), (1, 0), (1, 2)):
            late_copy(k, target).wait_send()

    @pl.when(x == 2)
    def _():
        late_copy(0, 1).wait_send()

    @pl.when(t > 0)
    def _():
        for l in range(slots):
            img_copy(l).wait_send()


def solution(mesh):
    nt = mesh.shape["tile"]

    def on_device(source, anchors, counts, reflect, lateral_x, lateral_y):
        shots, _, rows, width = source.shape
        slots = reflect.shape[1]
        any_spec = pl.BlockSpec(memory_space=pltpu.HBM)
        wave = (shots, 2 * rows, width)
        dma = pltpu.SemaphoreType.DMA
        return pl.pallas_call(
            functools.partial(kernel, nt),
            out_shape=jax.ShapeDtypeStruct((1, slots, rows, width), F32),
            in_specs=[any_spec] * 6,
            out_specs=pl.BlockSpec(memory_space=pltpu.VMEM),
            scratch_shapes=[
                pltpu.SMEM((shots,), jnp.int32),
                pltpu.SMEM((1,), jnp.int32),
                pltpu.VMEM((slots, rows, width), BF16),
                pltpu.VMEM((slots, rows, width), BF16),
                pltpu.VMEM((slots, 2, rows, rows), BF16),
                pltpu.VMEM((slots, 2, width, width), BF16),
                pltpu.VMEM((slots, 2 * rows, 2 * rows), BF16),
                pltpu.VMEM((slots, 2 * rows, 2 * rows), BF16),
                pltpu.VMEM((shots, width, width), BF16),
                pltpu.VMEM((shots, width, width), BF16),
                pltpu.VMEM((shots, slots, rows, width), F32),
                pltpu.VMEM((shots, slots + 1, 2 * rows, width), BF16),
                pltpu.VMEM(wave, BF16),
                pltpu.VMEM(wave, BF16),
                pltpu.VMEM(wave, BF16),
                pltpu.VMEM((2 * rows, 2 * rows), BF16),
                pltpu.VMEM((2, width, width), BF16),
                pltpu.VMEM((2 * rows, 2 * rows), BF16),
                pltpu.VMEM((2, width, width), BF16),
                pltpu.VMEM((2 * rows, 2 * rows), BF16),
                pltpu.VMEM((2, width, width), BF16),
                pltpu.VMEM((2 * rows, 2 * rows), BF16),
                pltpu.VMEM((2, width, width), BF16),
                pltpu.VMEM((shots, slots, 2 * rows, width), BF16),
                pltpu.VMEM((slots, rows, width), F32),
                pltpu.VMEM((shots, slots, rows, width), BF16),
                pltpu.VMEM((slots, rows, width), BF16),
                pltpu.VMEM((slots, rows, width), BF16),
                dma((5 + shots,)),
                dma((slots,)), dma((slots,)),
                dma((shots,)), dma((shots,)),
                dma((shots, 3)), dma((shots,)),
                dma((shots,)), dma((shots,)),
                dma((2, 2)), dma((2,)),
                dma((2,)), dma((2,)),
                dma((slots,)), dma((slots,)),
            ],
            compiler_params=pltpu.CompilerParams(
                collective_id=0, has_side_effects=True, vmem_limit_bytes=16 * 1024 * 1024
            ),
        )(in_hbm(source.reshape(wave)), in_hbm(anchors), counts, in_hbm(reflect), in_hbm(lateral_x), in_hbm(lateral_y))

    return jax.shard_map(
        on_device,
        mesh=mesh,
        in_specs=(
            P("tile", None, None, None),
            P("tile"),
            P("depth"),
            P("depth", None, None, "tile"),
            P("depth", None, None, None, None),
            P("depth", None, None, None, None),
        ),
        out_specs=P("depth", None, None, "tile"),
        check_vma=False,
    )
```

```python
import functools

import jax
import jax.numpy as jnp
from jax import lax
from jax.experimental import pallas as pl
from jax.experimental.pallas import tpu as pltpu
from jax.sharding import PartitionSpec as P

MESH = pl.DeviceIdType.MESH
F32 = jnp.float32
BF16 = jnp.bfloat16


def dot_nn(a, b):
    return lax.dot_general(a, b, (((1,), (0,)), ((), ())), preferred_element_type=F32)


def dot_nt(a, b):
    return lax.dot_general(a, b, (((1,), (1,)), ((), ())), preferred_element_type=F32)


def in_hbm(array):
    return pltpu.with_memory_space_constraint(array, pltpu.HBM)


def complex_dot(a_re, a_im, b_re, b_im):
    re = dot_nn(a_re, b_re) - dot_nn(a_im, b_im)
    im = dot_nn(a_re, b_im) + dot_nn(a_im, b_re)
    return re.astype(BF16), im.astype(BF16)


def kernel(
    nt,
    source, anchors_hbm, counts_hbm, reflect, lx, ly, out,
    anchors, counts, refl_own, refl_left, lxv, yv, xb, xbt, sel_own, sel_left, win,
    waves, late, early, early_out, own_x, own_y, comp_x, comp_y, both_x, both_y,
    near_x, near_y, kept, left_acc, corr, img_out, img_in,
    local_sem, refl_send, refl_recv, down_send, down_recv, late_send, late_recv,
    early_send, early_recv, comp_send, comp_recv, near_send, near_recv,
    img_send, img_recv,
):
    slots, rows, width = refl_own.shape
    shots = waves.shape[0]
    x = lax.axis_index("depth")
    t = lax.axis_index("tile")

    def remote(src, dst, send, recv, target):
        return pltpu.make_async_remote_copy(
            src_ref=src, dst_ref=dst, send_sem=send, recv_sem=recv,
            device_id=target, device_id_type=MESH,
        )

    copies = [
        pltpu.make_async_copy(lx.at[0], lxv, local_sem.at[0]),
        pltpu.make_async_copy(reflect.at[0], refl_own, local_sem.at[1]),
        pltpu.make_async_copy(ly.at[0], yv, local_sem.at[2]),
        pltpu.make_async_copy(anchors_hbm, anchors, local_sem.at[3]),
        pltpu.make_async_copy(counts_hbm, counts, local_sem.at[4]),
    ]
    for i in (1, 3, 4, 0, 2):
        copies[i].start()

    barrier = pltpu.get_barrier_semaphore()
    neighbours = (
        (lax.rem(x + 2, 4), t), (x, lax.rem(t + 1, nt)), (x, lax.rem(t + nt - 1, nt)),
        (lax.rem(x + 1, 4), t), (lax.rem(x + 3, 4), t),
    )
    for neighbour in neighbours:
        pl.semaphore_signal(barrier, inc=1, device_id=neighbour, device_id_type=MESH)

    to_below = (jnp.minimum(x + 1, 3), t)
    to_above = (jnp.maximum(x - 1, 0), t)
    to_right = (x, jnp.minimum(t + 1, nt - 1))
    to_left = (x, jnp.maximum(t - 1, 0))

    def refl_copy(l):
        return remote(refl_own.at[l], refl_left.at[l], refl_send.at[l], refl_recv.at[l], to_right)

    def img_copy(l):
        return remote(img_out.at[l], img_in.at[l], img_send.at[l], img_recv.at[l], to_left)

    def down_copy(k):
        return remote(
            waves.at[k, slots], waves.at[k, 0], down_send.at[k], down_recv.at[k], to_below
        )

    def late_copy(k, target):
        sem = late_send.at[k, target]
        return remote(late.at[k], late_in.at[k], sem, late_recv.at[k], (target, t))

    def early_copy(k):
        return remote(early_out.at[k], early.at[k], early_send.at[k], early_recv.at[k], to_above)

    def comp_copies(target):
        return [
            remote(own_x, comp_x, comp_send.at[0, target], comp_recv.at[0], (target, t)),
            remote(own_y, comp_y, comp_send.at[1, target], comp_recv.at[1], (target, t)),
        ]

    def near_copies():
        return [
            remote(own_x, near_x, near_send.at[0], near_recv.at[0], to_above),
            remote(own_y, near_y, near_send.at[1], near_recv.at[1], to_above),
        ]

    late_in = late
    source_copies = [
        pltpu.make_async_copy(source.at[k], waves.at[k, 0], local_sem.at[5 + k])
        for k in range(shots)
    ]

    @pl.when(x == 0)
    def _():
        for copy in source_copies:
            copy.start()

    copies[1].wait()
    pl.semaphore_wait(barrier, 5)

    @pl.when(t < nt - 1)
    def _():
        for l in range(slots):
            refl_copy(l).start()

    j_r = lax.broadcasted_iota(jnp.int32, (width, width), 0)
    j_c = lax.broadcasted_iota(jnp.int32, (width, width), 1)
    copies[3].wait()
    for k in range(shots):
        offset = anchors[k] - (t - 1) * width
        sel_left[k] = (j_r - j_c == offset).astype(BF16)
        sel_own[k] = (j_r - j_c == offset - width).astype(BF16)
    copies[4].wait()
    level_count = counts[0]

    def live(l):
        return (level_count > l).astype(F32)

    i_r = lax.broadcasted_iota(jnp.int32, (rows, rows), 0)
    i_c = lax.broadcasted_iota(jnp.int32, (rows, rows), 1)
    eye_x = (i_r == i_c).astype(F32)
    copies[0].wait()
    for l in range(slots):
        x_re = lxv[l, 0].astype(F32)
        x_im = lxv[l, 1].astype(F32)
        if l > 0:
            x_re = x_re * live(l) + eye_x * (1.0 - live(l))
            x_im = x_im * live(l)
        xb[l, :rows, :rows] = x_re.astype(BF16)
        xb[l, :rows, rows:] = (-x_im).astype(BF16)
        xb[l, rows:, :rows] = x_im.astype(BF16)
        xb[l, rows:, rows:] = x_re.astype(BF16)

    def transpose_operators():
        for l in range(slots):
            x_ret = xb[l, :rows, :rows].astype(F32).T
            x_imt = xb[l, rows:, :rows].astype(F32).T
            xbt[l, :rows, :rows] = x_ret.astype(BF16)
            xbt[l, :rows, rows:] = (-x_imt).astype(BF16)
            xbt[l, rows:, :rows] = x_imt.astype(BF16)
            xbt[l, rows:, rows:] = x_ret.astype(BF16)

    copies[2].wait()
    eye_y = (j_r == j_c).astype(F32)
    for l in range(1, slots):
        yv[l, 0] = (yv[l, 0].astype(F32) * live(l) + eye_y * (1.0 - live(l))).astype(BF16)
        yv[l, 1] = (yv[l, 1].astype(F32) * live(l)).astype(BF16)
    for l in range(slots):
        for k in range(shots):
            win[k, l] = dot_nn(refl_own[l], sel_own[k]) * live(l)

    def finish_window(l, first_shot=True, others=True):
        @pl.when(t > 0)
        def _():
            if first_shot:
                refl_copy(l).wait_recv()
                win[0, l] += dot_nn(refl_left[l], sel_left[0]) * live(l)
            if others:
                for k in range(1, shots):
                    win[k, l] += dot_nn(refl_left[l], sel_left[k]) * live(l)

    def descend(k, with_windows=False, steps=slots):
        def level(l):
            if with_windows:
                finish_window(l, k == 0, k == 1)
            gain = 1.0 + win[k, l]
            scaled = jnp.concatenate(
                [
                    (gain * waves[k, l, :rows].astype(F32)).astype(BF16),
                    (gain * waves[k, l, rows:].astype(F32)).astype(BF16),
                ],
                axis=0,
            )
            middle = dot_nn(xb[l], scaled).astype(BF16)
            by_re = dot_nt(middle, yv[l, 0])
            by_im = dot_nt(middle, yv[l, 1])
            waves[k, l + 1, :rows] = (by_re[:rows] - by_im[rows:]).astype(BF16)
            waves[k, l + 1, rows:] = (by_im[:rows] + by_re[rows:]).astype(BF16)

        for l in range(steps):
            level(l)

    def ascend(wave, k, images=None, from_zero=False, last=False):
        def level(l):
            gain = win[k, l]
            d_re = waves[k, l, :rows].astype(F32)
            d_im = waves[k, l, rows:].astype(F32)
            if from_zero and l == slots - 1:
                u_re = (gain * d_re).astype(BF16)
                u_im = (gain * d_im).astype(BF16)
            else:
                back = dot_nn(xbt[l], wave[k]).astype(BF16)
                by_re = dot_nn(back, yv[l, 0])
                by_im = dot_nn(back, yv[l, 1])
                u_re = (gain * d_re + (by_re[:rows] - by_im[rows:])).astype(BF16)
                u_im = (gain * d_im + (by_im[:rows] + by_re[rows:])).astype(BF16)
            wave[k, :rows] = u_re
            wave[k, rows:] = u_im
            if images == "keep":
                kept[k, l, :rows] = u_re
                kept[k, l, rows:] = u_im
            if images == "place":
                product = (d_re * u_re.astype(F32) + d_im * u_im.astype(F32)) * live(l)
                corr[k, l] = product.astype(BF16)
                if last:
                    image_left(l, k)

        for l in reversed(range(slots)):
            level(l)
        if images == "place":
            for l in reversed(range(slots)):
                if last:
                    image_own(l, k)
                else:
                    image_first(l, k)

    def image_first(l, k):
        left_acc[l] = dot_nt(corr[k, l], sel_left[k])
        out[0, l] = dot_nt(corr[k, l], sel_own[k])

    def image_left(l, k):
        img_out[l] = (left_acc[l] + dot_nt(corr[k, l], sel_left[k])).astype(BF16)

        @pl.when(t > 0)
        def _():
            img_copy(l).start()

    def image_own(l, k):
        out[0, l] += dot_nt(corr[k, l], sel_own[k])

    def compose():
        own_x[...] = dot_nn(xbt[slots - 2], xbt[slots - 1]).astype(BF16)
        own_y[0], own_y[1] = yv[slots - 1, 0], yv[slots - 1, 1]
        for l in reversed(range(slots - 1)):
            if l < slots - 2:
                own_x[...] = dot_nn(xbt[l], own_x[...]).astype(BF16)
            own_y[0], own_y[1] = complex_dot(own_y[0], own_y[1], yv[l, 0], yv[l, 1])

    def carry_over(op_x, op_y, wave, held, k, into):
        back = dot_nn(op_x[...], wave[k]).astype(BF16)
        by_re = dot_nn(back, op_y[0])
        by_im = dot_nn(back, op_y[1])
        held_re = held[k, :rows].astype(F32)
        held_im = held[k, rows:].astype(F32)
        into[k, :rows] = (held_re + (by_re[:rows] - by_im[rows:])).astype(BF16)
        into[k, rows:] = (held_im + (by_im[:rows] + by_re[rows:])).astype(BF16)

    @pl.when(x == 0)
    def _():
        for k in range(shots):
            source_copies[k].wait()
            descend(k, True)
            down_copy(k).start()
        transpose_operators()
        for copy in near_copies() + comp_copies(0):
            copy.wait_recv()
        both_x[...] = dot_nn(near_x[...], comp_x[...]).astype(BF16)
        both_y[0], both_y[1] = complex_dot(comp_y[0], comp_y[1], near_y[0], near_y[1])
        for k in range(shots):
            early_copy(k).wait_recv()
            late_copy(k, 0).wait_recv()
            if k == 0:
                late_copy(0, 1).start()
            carry_over(both_x, both_y, late, early, k, early)
            ascend(early, k, "place", last=k == 1)

    @pl.when(x > 0)
    def _():
        transpose_operators()
        for l in range(slots):
            finish_window(l)

    @pl.when(x == 1)
    def _():
        compose()
        for copy in near_copies():
            copy.start()
        for k in range(shots):
            down_copy(k).wait_recv()
            descend(k)
            down_copy(k).start()
        for k in range(shots):
            ascend(early_out, k, from_zero=True)
        for k in range(shots):
            early_copy(k).wait_recv()
            carry_over(own_x, own_y, early, early_out, k, early_out)
            early_copy(k).start()
        for copy in comp_copies(1):
            copy.wait_recv()
        for k in reversed(range(shots)):
            late_copy(k, 1).wait_recv()
            carry_over(comp_x, comp_y, late, early, k, late)
            ascend(late, k, "place", last=k == 0)

    @pl.when(x == 2)
    def _():
        compose()
        for copy in comp_copies(1) + comp_copies(0):
            copy.start()
        for k in range(shots):
            down_copy(k).wait_recv()
            descend(k)
            down_copy(k).start()
            ascend(early_out, k, from_zero=True)
            early_copy(k).start()
        late_copy(0, 2).wait_recv()
        ascend(late, 0, "place")
        late_copy(1, 2).wait_recv()
        ascend(late, 1, "place", last=True)

    @pl.when(x == 3)
    def _():
        for k in range(shots):
            down_copy(k).wait_recv()
            descend(k, steps=slots - 1)
            ascend(late, k, "keep", from_zero=True)
            for target in ((0, 2), (1, 0, 2))[k]:
                late_copy(k, target).start()
        for l in reversed(range(slots)):
            for k in range(shots):
                product = waves[k, l].astype(F32) * kept[k, l].astype(F32)
                corr[k, l] = ((product[:rows] + product[rows:]) * live(l)).astype(BF16)
            image_first(l, 0)
            image_left(l, 1)
            image_own(l, 1)

    @pl.when(t < nt - 1)
    def _():
        for l in reversed(range(slots)):
            img_copy(l).wait_recv()
            out[0, l] += img_in[l].astype(F32)
        for l in range(slots):
            refl_copy(l).wait_send()

    @pl.when(x < 3)
    def _():
        for k in range(shots):
            down_copy(k).wait_send()

    @pl.when((x == 1) | (x == 2))
    def _():
        for k in range(shots):
            early_copy(k).wait_send()
    @pl.when(x == 1)
    def _():
        for copy in near_copies():
            copy.wait_send()

    @pl.when(x == 2)
    def _():
        for copy in comp_copies(1) + comp_copies(0):
            copy.wait_send()

    @pl.when(x == 3)
    def _():
        for k, target in ((0, 0), (0, 2), (1, 0), (1, 1), (1, 2)):
            late_copy(k, target).wait_send()

    @pl.when(x == 0)
    def _():
        late_copy(0, 1).wait_send()

    @pl.when(t > 0)
    def _():
        for l in range(slots):
            img_copy(l).wait_send()


def solution(mesh):
    nt = mesh.shape["tile"]

    def on_device(source, anchors, counts, reflect, lateral_x, lateral_y):
        shots, _, rows, width = source.shape
        slots = reflect.shape[1]
        any_spec = pl.BlockSpec(memory_space=pltpu.HBM)
        wave = (shots, 2 * rows, width)
        dma = pltpu.SemaphoreType.DMA
        return pl.pallas_call(
            functools.partial(kernel, nt),
            out_shape=jax.ShapeDtypeStruct((1, slots, rows, width), F32),
            in_specs=[any_spec] * 6,
            out_specs=pl.BlockSpec(memory_space=pltpu.VMEM),
            scratch_shapes=[
                pltpu.SMEM((shots,), jnp.int32),
                pltpu.SMEM((1,), jnp.int32),
                pltpu.VMEM((slots, rows, width), BF16),
                pltpu.VMEM((slots, rows, width), BF16),
                pltpu.VMEM((slots, 2, rows, rows), BF16),
                pltpu.VMEM((slots, 2, width, width), BF16),
                pltpu.VMEM((slots, 2 * rows, 2 * rows), BF16),
                pltpu.VMEM((slots, 2 * rows, 2 * rows), BF16),
                pltpu.VMEM((shots, width, width), BF16),
                pltpu.VMEM((shots, width, width), BF16),
                pltpu.VMEM((shots, slots, rows, width), F32),
                pltpu.VMEM((shots, slots + 1, 2 * rows, width), BF16),
                pltpu.VMEM(wave, BF16),
                pltpu.VMEM(wave, BF16),
                pltpu.VMEM(wave, BF16),
                pltpu.VMEM((2 * rows, 2 * rows), BF16),
                pltpu.VMEM((2, width, width), BF16),
                pltpu.VMEM((2 * rows, 2 * rows), BF16),
                pltpu.VMEM((2, width, width), BF16),
                pltpu.VMEM((2 * rows, 2 * rows), BF16),
                pltpu.VMEM((2, width, width), BF16),
                pltpu.VMEM((2 * rows, 2 * rows), BF16),
                pltpu.VMEM((2, width, width), BF16),
                pltpu.VMEM((shots, slots, 2 * rows, width), BF16),
                pltpu.VMEM((slots, rows, width), F32),
                pltpu.VMEM((shots, slots, rows, width), BF16),
                pltpu.VMEM((slots, rows, width), BF16),
                pltpu.VMEM((slots, rows, width), BF16),
                dma((5 + shots,)),
                dma((slots,)), dma((slots,)),
                dma((shots,)), dma((shots,)),
                dma((shots, 3)), dma((shots,)),
                dma((shots,)), dma((shots,)),
                dma((2, 2)), dma((2,)),
                dma((2,)), dma((2,)),
                dma((slots,)), dma((slots,)),
            ],
            compiler_params=pltpu.CompilerParams(
                collective_id=0, has_side_effects=True, vmem_limit_bytes=16 * 1024 * 1024
            ),
        )(in_hbm(source.reshape(wave)), in_hbm(anchors), counts, in_hbm(reflect), in_hbm(lateral_x), in_hbm(lateral_y))

    return jax.shard_map(
        on_device,
        mesh=mesh,
        in_specs=(
            P("tile", None, None, None),
            P("tile"),
            P("depth"),
            P("depth", None, None, "tile"),
            P("depth", None, None, None, None),
            P("depth", None, None, None, None),
        ),
        out_specs=P("depth", None, None, "tile"),
        check_vma=False,
    )
```
